512 devices in a mesh: vol: 64 (over x, y, z_hi), src: 8 (over z_lo, core).
Axes of the slice: x: 4, y: 8, z: 8 (z_hi: 2, z_lo: 4; z = z_hi * 4 + z_lo), core: 2. Of those that a mesh axis runs over, the one named last changes fastest.
Arguments:
- excitation: float32 [32, 128, 128, 128], P(None, 'vol', 'src'), may hold values from -6 to 6
- start: float32 [32, 128, 128, 128], P(None, 'vol', 'src'), may hold values from -4 to 4
- material: int32 [128, 128, 128], P('vol', 'src'), may hold values from 0 to 2
- face_cell: int32 [64, 8, 256], P('vol', 'src'), may hold values from 0 to 4095
- face_count: int32 [64, 8, 64], P('vol', 'src'), may hold values from 0 to 4, as said below
- face_weight: float32 [64, 8, 256], P('vol', 'src'), may hold values from 0.5 to 1.5
- slot_panel: int32 [64, 8, 256], P('vol', 'src'), may hold values from 0 to 127
- target_points: float32 [3, 65536], P(None, 'vol'), may hold values from 0 to 1
- source_points: float32 [3, 65536], P(None, 'src'), may hold values from 0 to 1
Outputs:
- potential: float32 [32, 128, 128, 128], P(None, 'vol', 'src')
- flux: float32 [32, 65536], P(None, ('vol', 'src'))
The draws below stay inside these ranges and needn't reach their ends.
Inputs may be any that keep to these rules, and one draw needn't show every extreme that they name: A device has at most 4 live slots for one owner (the first face_count ones); in every draw some owner receives 4 live faces from every device.
All inputs are finite; a program needn't handle non-finite values.
Results may differ from the reference program's by a relative error of at most 0.0023.
The reference program's roundings to bfloat16 on the way (of `density` and `kernel`) count: a program that leaves them out, or rounds other values in their place, can miss the bound.
Values may be sent and summed in bfloat16 or wider, within the bound.
No kernel may reach another device: no remote copies, remote signals or barrier semaphores. Data moves between devices by JAX's collectives and lax.ppermute only.
A program may use at most 64 MiB of HBM per device.

```python
import jax
import jax.numpy as jnp
from jax import lax

EXC = 32
CX = 2
CY = 16
CZ = 128
P_SIZE = 65536
CAP = 4
ITERS = 2
SWEEPS = 2
NX = 128
NY = 128
NZ = 128
CELLS = 4096
PIECE = 128
N_VOL = 64
N_SRC = 8


def draw_face_count(key, part):
    limit_key = jax.random.fold_in(key, 11)
    spread_key = jax.random.fold_in(key, 12)
    full_key = jax.random.fold_in(key, 13)
    limit = jax.random.randint(limit_key, (N_VOL, N_SRC, 1), 1, CAP + 1)
    lowest = limit // 2
    raw_draw = jax.random.randint(spread_key, (N_VOL, N_SRC, N_VOL), 0, 1048576)
    counts = lowest + raw_draw % (limit - lowest + 1)
    full_owner = jax.random.randint(full_key, (), 0, N_VOL)
    owner_ids = jnp.arange(N_VOL, dtype=jnp.int32)[None, None, :]
    return jnp.where(owner_ids == full_owner, CAP, counts).astype(jnp.int32)


def touch_ends(values, stream_key, least, largest):
    longest = values.shape.index(max(values.shape))
    spots = []
    for shift in (0, 1):
        where = [jax.random.randint(jax.random.fold_in(stream_key, axis), (), 0, length) for axis, length in enumerate(values.shape)]
        where[longest] = (where[longest] + shift) % values.shape[longest]
        spots.append(tuple(where))
    return values.at[spots[0]].set(least).at[spots[1]].set(largest)


def block_levels(key, dims, cuts, least, largest):
    def one(position, blocks):
        draws = jax.random.uniform(jax.random.fold_in(jax.random.fold_in(key, 6), position), (blocks,), jnp.float32, least / len(cuts), largest / len(cuts))
        return jnp.repeat(jnp.exp(draws), dims[position] // blocks).reshape((-1,) + (1,) * (len(dims) - position - 1))

    level = one(*cuts[0])
    for cut in cuts[1:]:
        level = level * one(*cut)
    return level


def normal_values(stream_key, extent, deviation, bound, cuts=(), held_as=jnp.bfloat16):
    gain = block_levels(stream_key, extent, cuts, -0.22, 0.18) if cuts else 1.0
    array = jax.random.normal(stream_key, extent, jnp.float32) * deviation * gain
    return jnp.minimum(jnp.maximum(array, -bound), bound).astype(held_as)


def setup_inputs(seed: int = 0) -> dict:
    seeds = jax.random.split(jax.random.key(seed), 10)
    excitation = normal_values(seeds[0], (EXC, NX, NY, NZ), 1.0, 6.0, ((1, 64), (2, 8)), jnp.float32)
    start = normal_values(seeds[1], (EXC, NX, NY, NZ), 0.5, 4.0, ((1, 64), (2, 8)), jnp.float32)
    material = touch_ends(jax.random.randint(seeds[2], (NX, NY, NZ), 0, 3), jax.random.fold_in(seeds[2], 1), 0, 2).astype(jnp.int32)
    face_cell = touch_ends(jax.random.randint(seeds[3], (N_VOL, N_SRC, N_VOL * CAP), 0, CELLS), jax.random.fold_in(seeds[3], 1), 0, CELLS - 1).astype(jnp.int32)
    face_count = draw_face_count(jax.random.fold_in(seeds[9], 71), 0)
    face_weight = jnp.clip(0.5 + 1.0 * jax.random.uniform(seeds[5], (N_VOL, N_SRC, N_VOL * CAP), jnp.float32) ** block_levels(seeds[5], (N_VOL, N_SRC, N_VOL * CAP), ((0, 64), (1, 8)), -0.2, 0.2), 0.5, 1.5)
    slot_panel = touch_ends(jax.random.randint(seeds[6], (N_VOL, N_SRC, N_VOL * CAP), 0, PIECE), jax.random.fold_in(seeds[6], 1), 0, PIECE - 1).astype(jnp.int32)
    target_points = jnp.clip(1.0 * jax.random.uniform(seeds[7], (3, P_SIZE), jnp.float32) ** block_levels(seeds[7], (3, P_SIZE), ((1, 64),), -0.2, 0.2), 0.0, 1.0)
    source_points = jnp.clip(1.0 * jax.random.uniform(seeds[8], (3, P_SIZE), jnp.float32) ** block_levels(seeds[8], (3, P_SIZE), ((1, 8),), -0.2, 0.2), 0.0, 1.0)
    return {"excitation": excitation, "start": start, "material": material, "face_cell": face_cell, "face_count": face_count, "face_weight": face_weight, "slot_panel": slot_panel, "target_points": target_points, "source_points": source_points}


NU_BASE = (1.0, 0.05, 0.4)
NU_SATURATION = (0.0, 0.9, 0.3)
RELAXATION = 0.8
SOFTENING = 0.05

def reluctivity(grad_sq, material):
    base_value = jnp.zeros(material.shape, jnp.float32)
    slope_value = jnp.zeros(material.shape, jnp.float32)
    for material_id in range(3):
        picked = material == material_id
        base_value = jnp.where(picked, NU_BASE[material_id], base_value)
        slope_value = jnp.where(picked, NU_SATURATION[material_id], slope_value)
    return base_value[None] + slope_value[None] * grad_sq / (1.0 + grad_sq)

def gradient_sq(padded):
    along_x = 0.5 * (padded[:, 2:, 1:-1, 1:-1] - padded[:, :-2, 1:-1, 1:-1])
    along_y = 0.5 * (padded[:, 1:-1, 2:, 1:-1] - padded[:, 1:-1, :-2, 1:-1])
    along_z = 0.5 * (padded[:, 1:-1, 1:-1, 2:] - padded[:, 1:-1, 1:-1, :-2])
    return along_x * along_x + along_y * along_y + along_z * along_z

def relax(padded, weights, diagonal, forcing):
    center = padded[:, 1:-1, 1:-1, 1:-1]
    neighbours = (padded[:, 2:, 1:-1, 1:-1], padded[:, :-2, 1:-1, 1:-1], padded[:, 1:-1, 2:, 1:-1], padded[:, 1:-1, :-2, 1:-1], padded[:, 1:-1, 1:-1, 2:], padded[:, 1:-1, 1:-1, :-2])
    applied = diagonal * center
    for weight, neighbour in zip(weights, neighbours):
        applied = applied - weight * neighbour
    return center + RELAXATION * (forcing - applied) / diagonal

def panel_flux(density_src, target_points, source_points):
    block_len = 512
    target_blocks = target_points.reshape(3, P_SIZE // block_len, block_len).transpose(1, 0, 2)

    def one_block(block_points):
        dist_sq = jnp.zeros((block_len, P_SIZE), jnp.float32)
        for component in range(3):
            offset = block_points[component][:, None] - source_points[component][None, :]
            dist_sq = dist_sq + offset * offset
        kernel = lax.rsqrt(dist_sq + SOFTENING * SOFTENING).astype(jnp.bfloat16)
        return jnp.dot(density_src, kernel.T, preferred_element_type=jnp.float32)
    flux_blocks = lax.map(one_block, target_blocks)
    return flux_blocks.transpose(1, 0, 2).reshape(EXC, P_SIZE)

def reference(excitation, start, material, face_cell, face_count, face_weight, slot_panel, target_points, source_points):
    vol_ids = jnp.arange(N_VOL, dtype=jnp.int32)[:, None, None]
    src_ids = jnp.arange(N_SRC, dtype=jnp.int32)[None, :, None]
    slot_ids = jnp.arange(N_VOL * CAP, dtype=jnp.int32)[None, None, :]
    owner_ids = slot_ids // CAP
    rank_ids = slot_ids % CAP
    local_x = face_cell // (CY * CZ)
    local_y = face_cell // CZ % CY
    local_z = face_cell % CZ
    cell_index = (((vol_ids * CX + local_x) * NY + src_ids * CY + local_y) * NZ + local_z).reshape(-1).astype(jnp.int32)
    live_count = jnp.take_along_axis(face_count, jnp.broadcast_to(owner_ids, face_cell.shape), axis=2)
    slot_scale = jnp.where(rank_ids < live_count, face_weight, 0.0).reshape(-1)
    panel_local = slot_panel[owner_ids, src_ids, vol_ids * CAP + rank_ids]
    panel_index = ((owner_ids * N_SRC + src_ids) * PIECE + panel_local).reshape(-1).astype(jnp.int32)
    potential = start
    flux = jnp.zeros((EXC, P_SIZE), jnp.float32)
    for outer_index in range(ITERS):
        padded = jnp.pad(potential, ((0, 0), (1, 1), (1, 1), (1, 1)))
        nu_cells = reluctivity(gradient_sq(padded), material)
        nu_pad = jnp.pad(nu_cells, ((0, 0), (1, 1), (1, 1), (1, 1)), mode='edge')
        weights = (0.5 * (nu_cells + nu_pad[:, 2:, 1:-1, 1:-1]), 0.5 * (nu_cells + nu_pad[:, :-2, 1:-1, 1:-1]), 0.5 * (nu_cells + nu_pad[:, 1:-1, 2:, 1:-1]), 0.5 * (nu_cells + nu_pad[:, 1:-1, :-2, 1:-1]), 0.5 * (nu_cells + nu_pad[:, 1:-1, 1:-1, 2:]), 0.5 * (nu_cells + nu_pad[:, 1:-1, 1:-1, :-2]))
        diagonal = weights[0] + weights[1] + weights[2] + weights[3] + weights[4] + weights[5]
        flat_potential = potential.reshape(EXC, -1)
        traces = flat_potential[:, cell_index] * slot_scale[None, :]
        density = jnp.zeros((EXC, P_SIZE), jnp.float32).at[:, panel_index].add(traces).astype(jnp.bfloat16)
        density_src = density.reshape(EXC, N_VOL, N_SRC, PIECE).transpose(0, 2, 1, 3).reshape(EXC, P_SIZE)
        flux = panel_flux(density_src, target_points, source_points) * float(P_SIZE) ** (-0.5)
        surface = jnp.zeros((EXC, NX * NY * NZ), jnp.float32).at[:, cell_index].add(flux[:, panel_index] * slot_scale[None, :])
        forcing = excitation + surface.reshape(excitation.shape)
        for sweep_index in range(SWEEPS):
            potential = relax(jnp.pad(potential, ((0, 0), (1, 1), (1, 1), (1, 1))), weights, diagonal, forcing)
    return (potential, flux)
```

```python
import jax
import jax.numpy as jnp
from jax import lax
from jax.experimental import pallas as pl
from jax.experimental.pallas import tpu as pltpu
from jax.sharding import Mesh
from jax.sharding import PartitionSpec as P

P_SIZE = 65536
ITERS = 2
NU_BASE = (1.0, 0.05, 0.4)
NU_SATURATION = (0.0, 0.9, 0.3)
RELAXATION = 0.8
SOFTENING = 0.05

F32 = jnp.float32
BF16 = jnp.bfloat16
NXY = 32
EH = 16
LX, LY, LZ = 4, 16, 128
KERNEL_VMEM = 60 << 20
VM = pl.BlockSpec(memory_space=pltpu.VMEM)
SM = pl.BlockSpec(memory_space=pltpu.SMEM)
PLANE = ("x", "y")
ROW = ("z", "c")


def sds(shape, dtype=F32):
    return jax.ShapeDtypeStruct(shape, dtype)


def call(body, out_shape, args, smem=(), scratch=(), flops=2_000_000, nbytes=2_000_000):
    return pl.pallas_call(
        body,
        out_shape=out_shape,
        in_specs=[SM if i in smem else VM for i in range(len(args))],
        out_specs=jax.tree.map(lambda _: VM, out_shape),
        scratch_shapes=list(scratch),
        compiler_params=pltpu.CompilerParams(vmem_limit_bytes=8 << 20),
        cost_estimate=pl.CostEstimate(flops=flops, bytes_accessed=nbytes, transcendentals=0),
    )(*args)


def split3(value):
    one = value.astype(BF16).astype(F32)
    rest = value - one
    two = rest.astype(BF16).astype(F32)
    return one, two, rest - two


def augmented(points, is_target):
    length = points.shape[1]
    shifted = jnp.concatenate([points - 0.5, jnp.zeros((5, length), F32)])
    norm = jnp.sum(shifted * shifted, axis=0, keepdims=True)
    if is_target:
        norm = norm + SOFTENING * SOFTENING
    norms = split3(norm)
    parts = split3(shifted)
    index = lax.broadcasted_iota(jnp.int32, (8, length), 0)
    first = 0 if is_target else 3
    extra = jnp.where(index < 6, 1.0, 0.0)
    for i in range(3):
        extra = jnp.where(index == first + i, norms[i], extra)
    rows = []
    for i in range(3):
        for j in range(3):
            rows.append(-2.0 * parts[i] if is_target else parts[j])
    return jnp.concatenate(rows + [extra, jnp.zeros((48, length), F32)])


def kernel_matrix_body(t_ref, s_ref, out_ref, turned_ref, aug_ref):
    @pl.when(pl.program_id(0) == 0)
    def _():
        aug_ref[...] = augmented(t_ref[...], True).astype(BF16)

    sources = augmented(s_ref[...], False)
    for i in range(4):
        pieces = [sources[:, (2 * i + k) * 128 : (2 * i + k + 1) * 128].T for k in range(2)]
        turned = jnp.concatenate(pieces).astype(BF16)
        at = slice(i * 256, (i + 1) * 256)
        turned_ref[at, :] = turned
        dist_sq = jnp.dot(turned, aug_ref[...], preferred_element_type=F32)
        out_ref[at, :] = lax.rsqrt(dist_sq).astype(BF16)


def kernel_matrix(targets, sources):
    return pl.pallas_call(
        kernel_matrix_body,
        grid=(8,),
        out_shape=(sds((8192, 1024), BF16), sds((8192, 128), BF16)),
        in_specs=[
            pl.BlockSpec((3, 1024), lambda i: (0, 0)),
            pl.BlockSpec((3, 1024), lambda i: (0, i)),
        ],
        out_specs=(
            pl.BlockSpec((1024, 1024), lambda i: (i, 0)),
            pl.BlockSpec((1024, 128), lambda i: (i, 0)),
        ),
        scratch_shapes=[pltpu.VMEM((128, 1024), BF16)],
        compiler_params=pltpu.CompilerParams(vmem_limit_bytes=KERNEL_VMEM),
        cost_estimate=pl.CostEstimate(
            flops=2_000_000_000, bytes_accessed=20_000_000, transcendentals=8_400_000
        ),
    )(targets, sources)


def density_body(arr, owner_hot, msg):
    turned = arr[...].T
    dens = []
    for wl in range(2):
        total = jnp.zeros((EH, 128), F32)
        for vl in range(2):
            q = vl * 2 + wl
            rows = turned[q * EH : (q + 1) * EH]
            parts = jnp.concatenate(split3(rows)).astype(BF16)
            found = jnp.dot(
                parts, owner_hot[q * 128 : (q + 1) * 128, :], preferred_element_type=F32
            )
            total = total + found[:EH] + found[EH : 2 * EH] + found[2 * EH :]
        dens.append(total)
    out = jnp.concatenate(dens).astype(BF16)
    for peer in range(NXY):
        msg[peer] = out


def flux_body(arr, t_ref, k0_ref, turned_ref, out_ref, aug_ref, acc_ref):
    step = pl.program_id(0)

    @pl.when(step == 0)
    def _():
        aug_ref[...] = augmented(t_ref[...], True).astype(BF16)
        acc_ref[...] = jnp.zeros_like(acc_ref)

    totals = [acc_ref[0], acc_ref[1]]
    for i in range(4):
        at = slice(i * 256, (i + 1) * 256)
        dens = jnp.concatenate([arr[i, :EH], arr[i, EH:]], axis=1)
        dist_sq = jnp.dot(turned_ref[at, :], aug_ref[...], preferred_element_type=F32)
        k1 = lax.rsqrt(dist_sq).astype(BF16)
        totals[0] = totals[0] + jnp.dot(dens, k0_ref[at, :], preferred_element_type=F32)
        totals[1] = totals[1] + jnp.dot(dens, k1, preferred_element_type=F32)
    for half in range(2):
        acc_ref[half] = totals[half]

    @pl.when(step == 7)
    def _():
        for half in range(2):
            for part in range(8):
                out_ref[part, half] = acc_ref[half, :, part * 128 : (part + 1) * 128] * (
                    float(P_SIZE) ** (-0.5)
                )


def partial_flux(arrived, targets, k0, turned):
    return pl.pallas_call(
        flux_body,
        grid=(8,),
        out_shape=sds((8, 2, EH, 128)),
        in_specs=[
            pl.BlockSpec((4, 2 * EH, 128), lambda i: (i, 0, 0)),
            pl.BlockSpec((3, 1024), lambda i: (0, 0)),
            pl.BlockSpec((1024, 1024), lambda i: (i, 0)),
            pl.BlockSpec((1024, 128), lambda i: (i, 0)),
        ],
        out_specs=pl.BlockSpec((8, 2, EH, 128), lambda i: (0, 0, 0, 0)),
        scratch_shapes=[pltpu.VMEM((128, 1024), BF16), pltpu.VMEM((2, EH, 1024), F32)],
        compiler_params=pltpu.CompilerParams(vmem_limit_bytes=KERNEL_VMEM),
        cost_estimate=pl.CostEstimate(
            flops=4_000_000_000, bytes_accessed=20_000_000, transcendentals=8_400_000
        ),
    )(arrived, targets, k0, turned)


def owner_body(flags_ref, parts_ref, owner_hot, flux_ref, msg_ref):
    total = parts_ref[0]
    for part in range(1, 8):
        total = total + parts_ref[part]
    flux_ref[...] = total
    swapped = flags_ref[4] == 1
    blocks = (
        jnp.where(swapped, total[1], total[0]),
        jnp.where(swapped, total[0], total[1]),
    )
    nt = (((1,), (1,)), ((), ()))
    out = jnp.zeros((128, 128), F32)
    for q in range(4):
        above_rows = [jnp.zeros((EH * q, 128), F32)] if q else []
        rows = jnp.concatenate(
            above_rows + [blocks[q % 2], jnp.zeros((128 - EH * (q + 1), 128), F32)]
        )
        for piece in split3(rows):
            out = out + lax.dot_general(
                owner_hot[q * 128 : (q + 1) * 128, :],
                piece.astype(BF16),
                nt,
                preferred_element_type=F32,
            )
    msg_ref[...] = out


def lane_iota():
    return lax.broadcasted_iota(jnp.int32, (EH, LZ), 1)


def below(value, lane, edge):
    return jnp.where(lane == 0, edge, pltpu.roll(value, 1, 1))


def above(value, lane, edge):
    return jnp.where(lane == LZ - 1, edge, pltpu.roll(value, LZ - 1, 1))


def nu_body(
    flags_ref, pot, xl, xh, yl, yh, mo, mxl, mxh, myl, myh, pp, nu, scale
):
    pp[2:6, 2:18] = pot[...]
    pp[0:2, 2:18] = xl[...].astype(F32)
    pp[6:8, 2:18] = xh[...].astype(F32)
    pp[1:7, 0:2] = yl[...].astype(F32)
    pp[1:7, 18:20] = yh[...].astype(F32)
    lane = lane_iota()

    def nu_at(x, y, ids):
        center = pp[x, y]
        gx = pp[x + 1, y] - pp[x - 1, y]
        gy = pp[x, y + 1] - pp[x, y - 1]
        gz = above(center, lane, 0.0) - below(center, lane, 0.0)
        grad_sq = 0.25 * (gx * gx + gy * gy + gz * gz)
        base = jnp.where(ids == 0, NU_BASE[0], jnp.where(ids == 1, NU_BASE[1], NU_BASE[2]))
        slope = jnp.where(
            ids == 0, NU_SATURATION[0], jnp.where(ids == 1, NU_SATURATION[1], NU_SATURATION[2])
        )
        return base + slope * (grad_sq / (1.0 + grad_sq))

    def own_rows(y, carry):
        for x in range(LX):
            nu[x + 1, y + 1] = nu_at(x + 2, y + 2, mo[x, pl.ds(y, 1), :])
        nu[0, y + 1] = jnp.where(
            flags_ref[0] == 1, nu[1, y + 1], nu_at(1, y + 2, mxl[pl.ds(y, 1), :])
        )
        nu[5, y + 1] = jnp.where(
            flags_ref[1] == 1, nu[4, y + 1], nu_at(6, y + 2, mxh[pl.ds(y, 1), :])
        )
        return carry

    lax.fori_loop(0, LY, own_rows, 0)
    for x in range(LX):
        nu[x + 1, 0] = jnp.where(
            flags_ref[2] == 1, nu[x + 1, 1], nu_at(x + 2, 1, myl[x : x + 1, :])
        )
        nu[x + 1, 17] = jnp.where(
            flags_ref[3] == 1, nu[x + 1, 16], nu_at(x + 2, 18, myh[x : x + 1, :])
        )

    def scale_rows(y, carry):
        for x in range(LX):
            own = nu[x + 1, y + 1]
            total = (
                nu[x, y + 1]
                + nu[x + 2, y + 1]
                + nu[x + 1, y]
                + nu[x + 1, y + 2]
                + below(own, lane, own)
                + above(own, lane, own)
            )
            scale[x, y] = RELAXATION / (3.0 * own + 0.5 * total)
        return carry

    lax.fori_loop(0, LY, scale_rows, 0)


def relaxed(p, px, py, nu, scale, forcing, x, y, lane):
    center = p[x + px, y + py]
    own = nu[x + 1, y + 1]
    around = (
        (p[x + px - 1, y + py], nu[x, y + 1]),
        (p[x + px + 1, y + py], nu[x + 2, y + 1]),
        (p[x + px, y + py - 1], nu[x + 1, y]),
        (p[x + px, y + py + 1], nu[x + 1, y + 2]),
        (below(center, lane, 0.0), pltpu.roll(own, 1, 1)),
        (above(center, lane, 0.0), pltpu.roll(own, LZ - 1, 1)),
    )
    total = around[0][0] * (own + around[0][1])
    for value, other in around[1:]:
        total = total + value * (own + other)
    return (1.0 - RELAXATION) * center + scale[x, y] * (forcing + 0.5 * total)


def sweep_one_body(
    arr, hot, lanes_ref, exc, pp, nu, scale, pot, forcing, xlo, xhi, ylo, yhi
):
    turned = arr[...].T
    lane = lane_iota()
    slots = jnp.concatenate([turned[q * EH : (q + 1) * EH] for q in range(4)], axis=1)
    slots = slots * lanes_ref[1:2, :]
    hi = slots.astype(BF16).astype(F32)
    low = slots - hi
    cell_row = lanes_ref[0:1, :]
    for group in range(8):
        masks = [cell_row == float(group * 8 + i) for i in range(8)]
        surface = jnp.zeros((128, 128), F32)
        for piece in (hi, low):
            stacked = jnp.concatenate([jnp.where(m, piece, 0.0) for m in masks]).astype(BF16)
            surface = surface + jnp.dot(stacked, hot[...], preferred_element_type=F32)
        x = group // 2
        for i in range(8):
            y = (group % 2) * 8 + i
            forcing[x, y] = exc[x, y] + surface[i * EH : (i + 1) * EH]

    def rows(y, carry):
        for x in range(LX):
            pot[x, y] = relaxed(pp, 2, 2, nu, scale, forcing[x, y], x, y, lane)
        return carry

    lax.fori_loop(0, LY, rows, 0)
    xlo[...] = pot[0:1].astype(xlo.dtype)
    xhi[...] = pot[LX - 1 : LX].astype(xhi.dtype)
    ylo[...] = pot[:, 0:1].astype(ylo.dtype)
    yhi[...] = pot[:, LY - 1 : LY].astype(yhi.dtype)


def sweep_two_body(pot_in, xl, xh, yl, yh, nu, scale, forcing, pot, p):
    p[1:5, 1:17] = pot_in[...]
    p[0:1, 1:17] = xl[...].astype(F32)
    p[5:6, 1:17] = xh[...].astype(F32)
    p[1:5, 0:1] = yl[...].astype(F32)
    p[1:5, 17:18] = yh[...].astype(F32)
    lane = lane_iota()

    def rows(y, carry):
        for x in range(LX):
            pot[x, y] = relaxed(p, 1, 1, nu, scale, forcing[x, y], x, y, lane)
        return carry

    lax.fori_loop(0, LY, rows, 0)


def gather_traces(pot, hot, rows_ref, weight_ref, msg):
    nt = (((1,), (1,)), ((), ()))
    taken = jnp.zeros((512, 128), F32)
    for group in range(8):
        x, y = group // 2, (group % 2) * 8
        block = pot[x, y : y + 8].reshape(128, LZ)
        value = jnp.zeros((512, 128), F32)
        for piece in split3(block):
            value = value + lax.dot_general(
                hot[...], piece.astype(BF16), nt, preferred_element_type=F32
            )
        taken = jnp.where(rows_ref[...] == float(group * 8), value, taken)
    taken = taken * weight_ref[...]
    for shift_by in (64, 32, 16):
        taken = taken + pltpu.roll(taken, shift_by, 1)
    lane_group = lax.broadcasted_iota(jnp.int32, (128, 128), 1) // EH
    out = jnp.zeros((128, 128), F32)
    for q in range(4):
        out = jnp.where(lane_group == q, taken[q * 128 : (q + 1) * 128], out)
    msg[...] = out


def tables_gather_body(
    flags_ref, own, other, pot, msg, hot, rows_ref, weight_ref, owner_hot, lanes_ref
):
    swapped = flags_ref[4] == 1
    first = jnp.where(swapped, other[...], own[...])
    second = jnp.where(swapped, own[...], other[...])
    lane = lax.broadcasted_iota(jnp.int32, (128, 128), 1)
    lane_f = lane.astype(F32)
    group_f = (lane // EH).astype(F32)

    def column(row):
        return jnp.broadcast_to(row, (128, 128)).T

    for vl, table in enumerate((first, second)):
        for wl in range(2):
            q = vl * 2 + wl
            at = slice(q * 128, (q + 1) * 128)
            cell_row = jnp.floor(table[wl : wl + 1] * (1.0 / LZ))
            depth = table[wl : wl + 1] - cell_row * LZ
            cell_row = cell_row + 32.0 * vl
            lanes_ref[:, at] = jnp.concatenate(
                [cell_row, table[2 + wl : 3 + wl], jnp.zeros((6, 128), F32)]
            )
            hot[at, :] = jnp.where(column(depth) == lane_f, 1.0, 0.0).astype(BF16)
            rows_ref[at, :] = column(cell_row) - group_f
            weight_ref[at, :] = column(table[2 + wl : 3 + wl])
            owned = (first, second)[wl][4 + vl : 5 + vl]
            owner_hot[at, :] = jnp.where(column(owned) == lane_f, 1.0, 0.0).astype(BF16)
    gather_traces(pot, hot, rows_ref, weight_ref, msg)


def sweep_two_gather_body(
    pot_in, xl, xh, yl, yh, nu, scale, forcing, hot, rows_ref, weight_ref, pot, msg, p
):
    sweep_two_body(pot_in, xl, xh, yl, yh, nu, scale, forcing, pot, p)
    gather_traces(pot, hot, rows_ref, weight_ref, msg)


def shift(value, axes, count, step):
    pairs = [(i, i + step) for i in range(count) if 0 <= i + step < count]
    return lax.ppermute(value, axes, pairs)


def swap_h(value):
    return lax.ppermute(value, "h", [(0, 1), (1, 0)])


def by_h(h, own, other):
    return jnp.where(h == 0, jnp.concatenate([own, other]), jnp.concatenate([other, own]))


def halved(value, h):
    turned = value.transpose(1, 2, 0, 3)
    low, high = turned[:, :, :EH], turned[:, :, EH:]
    return jnp.where(h == 0, low, high), jnp.where(h == 0, high, low)


def per_device(
    excitation,
    start,
    material,
    face_cell,
    face_count,
    face_weight,
    slot_panel,
    target_points,
    source_points,
):
    h = lax.axis_index("h")
    plane = lax.axis_index(PLANE)
    row = lax.axis_index(ROW)
    flags = jnp.stack(
        [plane == 0, plane == NXY - 1, row == 0, row == 7, h == 1, h == 1, h == 1, h == 1]
    ).astype(jnp.int32)

    rank = jnp.arange(4, dtype=jnp.int32)[None, :]
    weight = jnp.where(
        rank < face_count.reshape(64, 1), face_weight.reshape(64, 4), 0.0
    ).reshape(256)
    tables = jnp.stack(
        [face_cell.reshape(256).astype(F32), weight, slot_panel.reshape(256).astype(F32)]
    )
    tables = tables.reshape(3, 32, 2, 4).transpose(0, 2, 1, 3).reshape(6, 128)
    tables = jnp.concatenate([tables, jnp.zeros((2, 128), F32)])
    keep, give = halved(start, h)
    got = swap_h(
        jnp.concatenate(
            [
                give.reshape(512, 128),
                tables,
                target_points.reshape(24, 128),
                material.reshape(32, 128).astype(F32),
            ]
        )
    )
    exc_keep, exc_give = halved(excitation, h)
    exc_got = swap_h(exc_give)
    k0, turned = kernel_matrix(target_points, source_points)

    pot = by_h(h, keep, got[:512].reshape(2, LY, EH, LZ))
    mats = by_h(h, material.astype(F32), got[544:576].reshape(2, LY, LZ))
    msg, hot, rows_col, weights_col, owner_hot, lanes = call(
        tables_gather_body,
        (
            sds((128, 128)),
            sds((512, 128), BF16),
            sds((512, 128)),
            sds((512, 128)),
            sds((512, 128), BF16),
            sds((8, 512)),
        ),
        (flags, tables, got[512:520], pot),
        smem=(0,),
    )
    their_targets = got[520:544].reshape(3, 1024)
    exc = by_h(h, exc_keep, exc_got)

    rims = None
    for outer_index in range(ITERS):
        arrived = lax.all_to_all(msg.reshape(NXY, 4, 128), PLANE, 0, 0, tiled=True)
        dens = call(
            density_body, sds((NXY, 2 * EH, 128), BF16), (arrived.reshape(128, 128), owner_hot)
        )
        dens = lax.all_to_all(dens, PLANE, 0, 0, tiled=True)

        coarse = pot.astype(BF16)
        up, down = coarse[2:4].reshape(512, 128), coarse[0:2].reshape(512, 128)
        if outer_index == 0:
            up = jnp.concatenate([up, mats[3].astype(BF16)])
            down = jnp.concatenate([down, mats[0].astype(BF16)])
        xl = shift(up, PLANE, NXY, 1)
        xh = shift(down, PLANE, NXY, -1)
        xl_pot = xl[:512].reshape(2, LY, EH, LZ)
        xh_pot = xh[:512].reshape(2, LY, EH, LZ)

        def side(part):
            rows = jnp.concatenate([xl_pot[1:2, part], coarse[:, part], xh_pot[0:1, part]])
            return rows.reshape(6 * 2 * EH, LZ)

        up, down = side(slice(14, 16)), side(slice(0, 2))
        if outer_index == 0:
            pad = jnp.zeros((12, 128), BF16)
            up = jnp.concatenate([up, mats[:, 15].astype(BF16), pad])
            down = jnp.concatenate([down, mats[:, 0].astype(BF16), pad])
        yl = shift(up, ROW, 8, 1)
        yh = shift(down, ROW, 8, -1)
        if outer_index == 0:
            rims = tuple(v.astype(F32) for v in (xl[512:], xh[512:], yl[192:], yh[192:]))
        padded, nu, scale = call(
            nu_body,
            (sds((8, 20, EH, LZ)), sds((6, 18, EH, LZ)), sds((LX, LY, EH, LZ))),
            (
                flags,
                pot,
                xl_pot,
                xh_pot,
                yl[:192].reshape(6, 2, EH, LZ),
                yh[:192].reshape(6, 2, EH, LZ),
                mats,
                *rims,
            ),
            smem=(0,),
        )

        parts = partial_flux(dens, their_targets, k0, turned)
        parts = lax.all_to_all(parts, ROW, 0, 0, tiled=True)
        flux, slots = call(
            owner_body, (sds((2, EH, 128)), sds((128, 128))), (flags, parts, owner_hot), smem=(0,)
        )
        back = lax.all_to_all(slots.reshape(NXY, 4, 128), PLANE, 0, 0, tiled=True)

        brick = (LX, LY, EH, LZ)
        pot, forcing, xlo, xhi, ylo, yhi = call(
            sweep_one_body,
            (
                sds(brick),
                sds(brick),
                sds((1, LY, EH, LZ), BF16),
                sds((1, LY, EH, LZ), BF16),
                sds((LX, 1, EH, LZ), BF16),
                sds((LX, 1, EH, LZ), BF16),
            ),
            (back.reshape(128, 128), hot, lanes, exc, padded, nu, scale),
        )
        xl1 = shift(xhi, PLANE, NXY, 1)
        xh1 = shift(xlo, PLANE, NXY, -1)
        yl1 = shift(yhi, ROW, 8, 1)
        yh1 = shift(ylo, ROW, 8, -1)
        operands = (pot, xl1, xh1, yl1, yh1, nu, scale, forcing)
        scratch = (pltpu.VMEM((6, 18, EH, LZ), F32),)
        if outer_index < ITERS - 1:
            pot, msg = call(
                sweep_two_gather_body,
                (sds(brick), sds((128, 128))),
                operands + (hot, rows_col, weights_col),
                scratch=scratch,
            )
        else:
            pot = call(sweep_two_body, sds(brick), operands, scratch=scratch)

    lower, upper = pot[0:2], pot[2:4]
    mine = jnp.where(h == 0, lower, upper)
    theirs = jnp.where(h == 0, upper, lower)
    final = swap_h(jnp.concatenate([theirs.reshape(512, 128), flux[1]]))
    theirs = final[:512].reshape(2, LY, EH, LZ)
    out = jnp.where(
        h == 0, jnp.concatenate([mine, theirs], axis=2), jnp.concatenate([theirs, mine], axis=2)
    )
    flux_out = by_h(h, flux[0], final[512:])
    return out.transpose(2, 0, 1, 3), flux_out


def solution(mesh):
    fine = Mesh(mesh.devices.reshape(4, 8, 2, 4, 2), ("x", "y", "h", "z", "c"))
    vol, src = ("x", "y", "h"), ("z", "c")
    return jax.shard_map(
        per_device,
        mesh=fine,
        in_specs=(
            P(None, vol, src, None),
            P(None, vol, src, None),
            P(vol, src, None),
            P(vol, src, None),
            P(vol, src, None),
            P(vol, src, None),
            P(vol, src, None),
            P(None, vol),
            P(None, src),
        ),
        out_specs=(P(None, vol, src, None), P(None, vol + src)),
        check_vma=False,
    )
```

```python
import jax
import jax.numpy as jnp
from jax import lax
from jax.experimental import pallas as pl
from jax.experimental.pallas import tpu as pltpu
from jax.sharding import Mesh
from jax.sharding import PartitionSpec as P

P_SIZE = 65536
ITERS = 2
NU_BASE = (1.0, 0.05, 0.4)
NU_SATURATION = (0.0, 0.9, 0.3)
RELAXATION = 0.8
SOFTENING = 0.05

F32 = jnp.float32
BF16 = jnp.bfloat16
NXY = 32
EH = 16
LX, LY, LZ = 4, 16, 128
KERNEL_VMEM = 60 << 20
VM = pl.BlockSpec(memory_space=pltpu.VMEM)
SM = pl.BlockSpec(memory_space=pltpu.SMEM)
PLANE = ("x", "y")
ROW = ("z", "c")


def sds(shape, dtype=F32):
    return jax.ShapeDtypeStruct(shape, dtype)


def call(body, out_shape, args, smem=(), scratch=(), flops=2_000_000, nbytes=2_000_000):
    return pl.pallas_call(
        body,
        out_shape=out_shape,
        in_specs=[SM if i in smem else VM for i in range(len(args))],
        out_specs=jax.tree.map(lambda _: VM, out_shape),
        scratch_shapes=list(scratch),
        compiler_params=pltpu.CompilerParams(vmem_limit_bytes=8 << 20),
        cost_estimate=pl.CostEstimate(flops=flops, bytes_accessed=nbytes, transcendentals=0),
    )(*args)


def split3(value):
    one = value.astype(BF16).astype(F32)
    rest = value - one
    two = rest.astype(BF16).astype(F32)
    return one, two, rest - two


def augmented(points, is_target):
    length = points.shape[1]
    shifted = jnp.concatenate([points - 0.5, jnp.zeros((5, length), F32)])
    norm = jnp.sum(shifted * shifted, axis=0, keepdims=True)
    if is_target:
        norm = norm + SOFTENING * SOFTENING
    norms = split3(norm)
    parts = split3(shifted)
    index = lax.broadcasted_iota(jnp.int32, (8, length), 0)
    first = 0 if is_target else 3
    extra = jnp.where(index < 6, 1.0, 0.0)
    for i in range(3):
        extra = jnp.where(index == first + i, norms[i], extra)
    rows = []
    for i in range(3):
        for j in range(3):
            rows.append(-2.0 * parts[i] if is_target else parts[j])
    return jnp.concatenate(rows + [extra, jnp.zeros((48, length), F32)])


def kernel_matrix_body(t_ref, s_ref, out_ref, turned_ref, aug_ref):
    @pl.when(pl.program_id(0) == 0)
    def _():
        aug_ref[...] = augmented(t_ref[...], True).astype(BF16)

    sources = augmented(s_ref[...], False)
    for i in range(4):
        pieces = [sources[:, (2 * i + k) * 128 : (2 * i + k + 1) * 128].T for k in range(2)]
        turned = jnp.concatenate(pieces).astype(BF16)
        at = slice(i * 256, (i + 1) * 256)
        turned_ref[at, :] = turned
        dist_sq = jnp.dot(turned, aug_ref[...], preferred_element_type=F32)
        out_ref[at, :] = lax.rsqrt(dist_sq).astype(BF16)


def kernel_matrix(targets, sources):
    return pl.pallas_call(
        kernel_matrix_body,
        grid=(8,),
        out_shape=(sds((8192, 1024), BF16), sds((8192, 128), BF16)),
        in_specs=[
            pl.BlockSpec((3, 1024), lambda i: (0, 0)),
            pl.BlockSpec((3, 1024), lambda i: (0, i)),
        ],
        out_specs=(
            pl.BlockSpec((1024, 1024), lambda i: (i, 0)),
            pl.BlockSpec((1024, 128), lambda i: (i, 0)),
        ),
        scratch_shapes=[pltpu.VMEM((128, 1024), BF16)],
        compiler_params=pltpu.CompilerParams(vmem_limit_bytes=KERNEL_VMEM),
        cost_estimate=pl.CostEstimate(
            flops=2_000_000_000, bytes_accessed=20_000_000, transcendentals=8_400_000
        ),
    )(targets, sources)


def density_body(arr, owner_hot, msg):
    turned = arr[...].T
    dens = []
    for wl in range(2):
        total = jnp.zeros((EH, 128), F32)
        for vl in range(2):
            q = vl * 2 + wl
            rows = turned[q * EH : (q + 1) * EH]
            parts = jnp.concatenate(split3(rows)).astype(BF16)
            found = jnp.dot(
                parts, owner_hot[q * 128 : (q + 1) * 128, :], preferred_element_type=F32
            )
            total = total + found[:EH] + found[EH : 2 * EH] + found[2 * EH :]
        dens.append(total)
    out = jnp.concatenate(dens).astype(BF16)
    for peer in range(NXY):
        msg[peer] = out


FLUX_STEPS = 4
FLUX_ROWS = 8192 // FLUX_STEPS


def flux_body(arr, t_ref, ka, kb, kc, kd, turned_ref, out_ref, aug_ref, acc_ref):
    step = pl.program_id(0)

    @pl.when(step == 0)
    def _():
        aug_ref[...] = augmented(t_ref[...], True).astype(BF16)
        acc_ref[...] = jnp.zeros_like(acc_ref)

    pieces = []
    for i in range(FLUX_ROWS // 256):
        pieces += [arr[i, :EH], arr[i, EH:]]
    dens = jnp.concatenate(pieces, axis=1)
    depth = FLUX_ROWS // 4
    for c in range(2):
        at = slice(c * 512, (c + 1) * 512)
        dist_sq = jnp.dot(turned_ref[...], aug_ref[:, at], preferred_element_type=F32)
        k1 = lax.rsqrt(dist_sq).astype(BF16)
        acc_ref[1, :, at] += jnp.dot(dens, k1, preferred_element_type=F32)
        total = acc_ref[0, :, at]
        for part, k_ref in enumerate((ka, kb, kc, kd)):
            total = total + jnp.dot(
                dens[:, part * depth : (part + 1) * depth],
                k_ref[:, at],
                preferred_element_type=F32,
            )
        acc_ref[0, :, at] = total

    @pl.when(step == FLUX_STEPS - 1)
    def _():
        for half in range(2):
            for part in range(8):
                out_ref[part, half] = acc_ref[half, :, part * 128 : (part + 1) * 128] * (
                    float(P_SIZE) ** (-0.5)
                )


def stored_part(part):
    return pl.BlockSpec((FLUX_ROWS // 4, 1024), lambda i: (i * 4 + part, 0))


def partial_flux(arrived, targets, k0, turned):
    return pl.pallas_call(
        flux_body,
        grid=(FLUX_STEPS,),
        out_shape=sds((8, 2, EH, 128)),
        in_specs=[
            pl.BlockSpec((FLUX_ROWS // 256, 2 * EH, 128), lambda i: (i, 0, 0)),
            pl.BlockSpec((3, 1024), lambda i: (0, 0)),
            *[stored_part(part) for part in range(4)],
            pl.BlockSpec((FLUX_ROWS, 128), lambda i: (i, 0)),
        ],
        out_specs=pl.BlockSpec((8, 2, EH, 128), lambda i: (0, 0, 0, 0)),
        scratch_shapes=[pltpu.VMEM((128, 1024), BF16), pltpu.VMEM((2, EH, 1024), F32)],
        compiler_params=pltpu.CompilerParams(vmem_limit_bytes=KERNEL_VMEM),
        cost_estimate=pl.CostEstimate(
            flops=4_000_000_000, bytes_accessed=20_000_000, transcendentals=8_400_000
        ),
    )(arrived, targets, k0, k0, k0, k0, turned)


def owner_body(flags_ref, parts_ref, owner_hot, flux_ref, msg_ref):
    total = parts_ref[0]
    for part in range(1, 8):
        total = total + parts_ref[part]
    flux_ref[...] = total
    swapped = flags_ref[4] == 1
    blocks = (
        jnp.where(swapped, total[1], total[0]),
        jnp.where(swapped, total[0], total[1]),
    )
    nt = (((1,), (1,)), ((), ()))
    out = jnp.zeros((128, 128), F32)
    for q in range(4):
        above_rows = [jnp.zeros((EH * q, 128), F32)] if q else []
        rows = jnp.concatenate(
            above_rows + [blocks[q % 2], jnp.zeros((128 - EH * (q + 1), 128), F32)]
        )
        for piece in split3(rows):
            out = out + lax.dot_general(
                owner_hot[q * 128 : (q + 1) * 128, :],
                piece.astype(BF16),
                nt,
                preferred_element_type=F32,
            )
    msg_ref[...] = out


def lane_iota():
    return lax.broadcasted_iota(jnp.int32, (EH, LZ), 1)


def below(value, lane, edge):
    return jnp.where(lane == 0, edge, pltpu.roll(value, 1, 1))


def above(value, lane, edge):
    return jnp.where(lane == LZ - 1, edge, pltpu.roll(value, LZ - 1, 1))


def nu_body(
    flags_ref, pot, xl, xh, yl, yh, mo, mxl, mxh, myl, myh, nu, scale, pp
):
    pp[2:6, 2:18] = pot[...]
    pp[0:2, 2:18] = xl[...].astype(F32)
    pp[6:8, 2:18] = xh[...].astype(F32)
    pp[1:7, 0:2] = yl[...].astype(F32)
    pp[1:7, 18:20] = yh[...].astype(F32)
    lane = lane_iota()

    def nu_at(x, y, ids):
        center = pp[x, y]
        gx = pp[x + 1, y] - pp[x - 1, y]
        gy = pp[x, y + 1] - pp[x, y - 1]
        gz = above(center, lane, 0.0) - below(center, lane, 0.0)
        grad_sq = 0.25 * (gx * gx + gy * gy + gz * gz)
        base = jnp.where(ids == 0, NU_BASE[0], jnp.where(ids == 1, NU_BASE[1], NU_BASE[2]))
        slope = jnp.where(
            ids == 0, NU_SATURATION[0], jnp.where(ids == 1, NU_SATURATION[1], NU_SATURATION[2])
        )
        return base + slope * (grad_sq / (1.0 + grad_sq))

    def own_rows(y, carry):
        for x in range(LX):
            nu[x + 1, y + 1] = nu_at(x + 2, y + 2, mo[x, pl.ds(y, 1), :])
        nu[0, y + 1] = jnp.where(
            flags_ref[0] == 1, nu[1, y + 1], nu_at(1, y + 2, mxl[pl.ds(y, 1), :])
        )
        nu[5, y + 1] = jnp.where(
            flags_ref[1] == 1, nu[4, y + 1], nu_at(6, y + 2, mxh[pl.ds(y, 1), :])
        )
        return carry

    lax.fori_loop(0, LY, own_rows, 0)
    for x in range(LX):
        nu[x + 1, 0] = jnp.where(
            flags_ref[2] == 1, nu[x + 1, 1], nu_at(x + 2, 1, myl[x : x + 1, :])
        )
        nu[x + 1, 17] = jnp.where(
            flags_ref[3] == 1, nu[x + 1, 16], nu_at(x + 2, 18, myh[x : x + 1, :])
        )

    def scale_rows(y, carry):
        for x in range(LX):
            own = nu[x + 1, y + 1]
            total = (
                nu[x, y + 1]
                + nu[x + 2, y + 1]
                + nu[x + 1, y]
                + nu[x + 1, y + 2]
                + below(own, lane, own)
                + above(own, lane, own)
            )
            scale[x, y] = RELAXATION / (3.0 * own + 0.5 * total)
        return carry

    lax.fori_loop(0, LY, scale_rows, 0)


def relaxed(p, px, py, nu, scale, forcing, x, y, lane):
    center = p[x + px, y + py]
    own = nu[x + 1, y + 1]
    around = (
        (p[x + px - 1, y + py], nu[x, y + 1]),
        (p[x + px + 1, y + py], nu[x + 2, y + 1]),
        (p[x + px, y + py - 1], nu[x + 1, y]),
        (p[x + px, y + py + 1], nu[x + 1, y + 2]),
        (below(center, lane, 0.0), pltpu.roll(own, 1, 1)),
        (above(center, lane, 0.0), pltpu.roll(own, LZ - 1, 1)),
    )
    total = around[0][0] * (own + around[0][1])
    for value, other in around[1:]:
        total = total + value * (own + other)
    return (1.0 - RELAXATION) * center + scale[x, y] * (forcing + 0.5 * total)


def sweep_one_body(
    arr, hot, lanes_ref, exc, pot_in, xl, xh, yl, yh, nu, scale,
    pot, forcing, xlo, xhi, ylo, yhi, p,
):
    turned = arr[...].T
    lane = lane_iota()
    p[1:5, 1:17] = pot_in[...]
    p[0:1, 1:17] = xl[1:2].astype(F32)
    p[5:6, 1:17] = xh[0:1].astype(F32)
    p[1:5, 0:1] = yl[1:5, 1:2].astype(F32)
    p[1:5, 17:18] = yh[1:5, 0:1].astype(F32)
    slots = jnp.concatenate([turned[q * EH : (q + 1) * EH] for q in range(4)], axis=1)
    slots = slots * lanes_ref[1:2, :]
    hi = slots.astype(BF16).astype(F32)
    low = slots - hi
    cell_row = lanes_ref[0:1, :]
    for group in range(8):
        masks = [cell_row == float(group * 8 + i) for i in range(8)]
        surface = jnp.zeros((128, 128), F32)
        for piece in (hi, low):
            stacked = jnp.concatenate([jnp.where(m, piece, 0.0) for m in masks]).astype(BF16)
            surface = surface + jnp.dot(stacked, hot[...], preferred_element_type=F32)
        x = group // 2
        for i in range(8):
            y = (group % 2) * 8 + i
            forcing[x, y] = exc[x, y] + surface[i * EH : (i + 1) * EH]

    def rows(y, carry):
        for x in range(LX):
            pot[x, y] = relaxed(p, 1, 1, nu, scale, forcing[x, y], x, y, lane)
        return carry

    lax.fori_loop(0, LY, rows, 0)
    xlo[...] = pot[0:1].astype(xlo.dtype)
    xhi[...] = pot[LX - 1 : LX].astype(xhi.dtype)
    ylo[...] = pot[:, 0:1].astype(ylo.dtype)
    yhi[...] = pot[:, LY - 1 : LY].astype(yhi.dtype)


def sweep_two_body(pot_in, xl, xh, yl, yh, nu, scale, forcing, pot, p):
    p[1:5, 1:17] = pot_in[...]
    p[0:1, 1:17] = xl[...].astype(F32)
    p[5:6, 1:17] = xh[...].astype(F32)
    p[1:5, 0:1] = yl[...].astype(F32)
    p[1:5, 17:18] = yh[...].astype(F32)
    lane = lane_iota()

    def rows(y, carry):
        for x in range(LX):
            pot[x, y] = relaxed(p, 1, 1, nu, scale, forcing[x, y], x, y, lane)
        return carry

    lax.fori_loop(0, LY, rows, 0)


def gather_traces(pot, hot, rows_ref, weight_ref, msg):
    nt = (((1,), (1,)), ((), ()))
    taken = jnp.zeros((512, 128), F32)
    for group in range(8):
        x, y = group // 2, (group % 2) * 8
        block = pot[x, y : y + 8].reshape(128, LZ)
        value = jnp.zeros((512, 128), F32)
        for piece in split3(block):
            value = value + lax.dot_general(
                hot[...], piece.astype(BF16), nt, preferred_element_type=F32
            )
        taken = jnp.where(rows_ref[...] == float(group * 8), value, taken)
    taken = taken * weight_ref[...]
    for shift_by in (64, 32, 16):
        taken = taken + pltpu.roll(taken, shift_by, 1)
    lane_group = lax.broadcasted_iota(jnp.int32, (128, 128), 1) // EH
    out = jnp.zeros((128, 128), F32)
    for q in range(4):
        out = jnp.where(lane_group == q, taken[q * 128 : (q + 1) * 128], out)
    msg[...] = out


def tables_gather_body(
    flags_ref, own, other, pot, msg, hot, rows_ref, weight_ref, owner_hot, lanes_ref
):
    swapped = flags_ref[4] == 1
    first = jnp.where(swapped, other[...], own[...])
    second = jnp.where(swapped, own[...], other[...])
    lane = lax.broadcasted_iota(jnp.int32, (128, 128), 1)
    lane_f = lane.astype(F32)
    group_f = (lane // EH).astype(F32)

    def column(row):
        return jnp.broadcast_to(row, (128, 128)).T

    for vl, table in enumerate((first, second)):
        for wl in range(2):
            q = vl * 2 + wl
            at = slice(q * 128, (q + 1) * 128)
            cell_row = jnp.floor(table[wl : wl + 1] * (1.0 / LZ))
            depth = table[wl : wl + 1] - cell_row * LZ
            cell_row = cell_row + 32.0 * vl
            lanes_ref[:, at] = jnp.concatenate(
                [cell_row, table[2 + wl : 3 + wl], jnp.zeros((6, 128), F32)]
            )
            hot[at, :] = jnp.where(column(depth) == lane_f, 1.0, 0.0).astype(BF16)
            rows_ref[at, :] = column(cell_row) - group_f
            weight_ref[at, :] = column(table[2 + wl : 3 + wl])
            owned = (first, second)[wl][4 + vl : 5 + vl]
            owner_hot[at, :] = jnp.where(column(owned) == lane_f, 1.0, 0.0).astype(BF16)
    gather_traces(pot, hot, rows_ref, weight_ref, msg)


def sweep_two_gather_body(
    pot_in, xl, xh, yl, yh, nu, scale, forcing, hot, rows_ref, weight_ref, pot, msg, p
):
    sweep_two_body(pot_in, xl, xh, yl, yh, nu, scale, forcing, pot, p)
    gather_traces(pot, hot, rows_ref, weight_ref, msg)


def shift(value, axes, count, step):
    pairs = [(i, i + step) for i in range(count) if 0 <= i + step < count]
    return lax.ppermute(value, axes, pairs)


def swap_h(value):
    return lax.ppermute(value, "h", [(0, 1), (1, 0)])


def by_h(h, own, other):
    return jnp.where(h == 0, jnp.concatenate([own, other]), jnp.concatenate([other, own]))


def halved(value, h):
    turned = value.transpose(1, 2, 0, 3)
    low, high = turned[:, :, :EH], turned[:, :, EH:]
    return jnp.where(h == 0, low, high), jnp.where(h == 0, high, low)


def per_device(
    excitation,
    start,
    material,
    face_cell,
    face_count,
    face_weight,
    slot_panel,
    target_points,
    source_points,
):
    h = lax.axis_index("h")
    plane = lax.axis_index(PLANE)
    row = lax.axis_index(ROW)
    flags = jnp.stack(
        [plane == 0, plane == NXY - 1, row == 0, row == 7, h == 1, h == 1, h == 1, h == 1]
    ).astype(jnp.int32)

    rank = jnp.arange(4, dtype=jnp.int32)[None, :]
    weight = jnp.where(
        rank < face_count.reshape(64, 1), face_weight.reshape(64, 4), 0.0
    ).reshape(256)
    tables = jnp.stack(
        [face_cell.reshape(256).astype(F32), weight, slot_panel.reshape(256).astype(F32)]
    )
    tables = tables.reshape(3, 32, 2, 4).transpose(0, 2, 1, 3).reshape(6, 128)
    tables = jnp.concatenate([tables, jnp.zeros((2, 128), F32)])
    keep, give = halved(start, h)
    got = swap_h(
        jnp.concatenate(
            [
                give.reshape(512, 128),
                tables,
                target_points.reshape(24, 128),
                material.reshape(32, 128).astype(F32),
            ]
        )
    )
    k0, turned = kernel_matrix(target_points, source_points)

    pot = by_h(h, keep, got[:512].reshape(2, LY, EH, LZ))
    mats = by_h(h, material.astype(F32), got[544:576].reshape(2, LY, LZ))
    msg, hot, rows_col, weights_col, owner_hot, lanes = call(
        tables_gather_body,
        (
            sds((128, 128)),
            sds((512, 128), BF16),
            sds((512, 128)),
            sds((512, 128)),
            sds((512, 128), BF16),
            sds((8, 512)),
        ),
        (flags, tables, got[512:520], pot),
        smem=(0,),
    )
    their_targets = got[520:544].reshape(3, 1024)

    rims = None
    for outer_index in range(ITERS):
        msg, coarse = lax.optimization_barrier((msg, pot))
        coarse = coarse.astype(BF16)
        arrived = lax.all_to_all(msg.reshape(NXY, 4, 128), PLANE, 0, 0, tiled=True)
        dens = call(
            density_body, sds((NXY, 2 * EH, 128), BF16), (arrived.reshape(128, 128), owner_hot)
        )
        if outer_index == 0:
            dens, late = lax.optimization_barrier((dens, excitation))
            exc_keep, exc_give = halved(late, h)
            exc = by_h(h, exc_keep, swap_h(exc_give))
        dens = lax.all_to_all(dens, PLANE, 0, 0, tiled=True)

        up, down = coarse[2:4].reshape(512, 128), coarse[0:2].reshape(512, 128)
        if outer_index == 0:
            up = jnp.concatenate([up, mats[3].astype(BF16)])
            down = jnp.concatenate([down, mats[0].astype(BF16)])
        xl = shift(up, PLANE, NXY, 1)
        xh = shift(down, PLANE, NXY, -1)
        xl_pot = xl[:512].reshape(2, LY, EH, LZ)
        xh_pot = xh[:512].reshape(2, LY, EH, LZ)

        def side(part):
            rows = jnp.concatenate([xl_pot[1:2, part], coarse[:, part], xh_pot[0:1, part]])
            return rows.reshape(6 * 2 * EH, LZ)

        up, down = side(slice(14, 16)), side(slice(0, 2))
        if outer_index == 0:
            pad = jnp.zeros((12, 128), BF16)
            up = jnp.concatenate([up, mats[:, 15].astype(BF16), pad])
            down = jnp.concatenate([down, mats[:, 0].astype(BF16), pad])
        yl = shift(up, ROW, 8, 1)
        yh = shift(down, ROW, 8, -1)
        if outer_index == 0:
            rims = tuple(v.astype(F32) for v in (xl[512:], xh[512:], yl[192:], yh[192:]))
        scratch = (pltpu.VMEM((6, 18, EH, LZ), F32),)
        halos = (
            xl_pot,
            xh_pot,
            yl[:192].reshape(6, 2, EH, LZ),
            yh[:192].reshape(6, 2, EH, LZ),
        )
        nu, scale = call(
            nu_body,
            (sds((6, 18, EH, LZ)), sds((LX, LY, EH, LZ))),
            (flags, pot, *halos, mats, *rims),
            smem=(0,),
            scratch=(pltpu.VMEM((8, 20, EH, LZ), F32),),
        )

        parts = partial_flux(dens, their_targets, k0, turned)
        parts = lax.all_to_all(parts, ROW, 0, 0, tiled=True)
        flux, slots = call(
            owner_body, (sds((2, EH, 128)), sds((128, 128))), (flags, parts, owner_hot), smem=(0,)
        )
        back = lax.all_to_all(slots.reshape(NXY, 4, 128), PLANE, 0, 0, tiled=True)

        brick = (LX, LY, EH, LZ)
        pot, forcing, xlo, xhi, ylo, yhi = call(
            sweep_one_body,
            (
                sds(brick),
                sds(brick),
                sds((1, LY, EH, LZ), BF16),
                sds((1, LY, EH, LZ), BF16),
                sds((LX, 1, EH, LZ), BF16),
                sds((LX, 1, EH, LZ), BF16),
            ),
            (back.reshape(128, 128), hot, lanes, exc, pot, *halos, nu, scale),
            scratch=scratch,
        )
        xl1 = shift(xhi, PLANE, NXY, 1)
        xh1 = shift(xlo, PLANE, NXY, -1)
        yl1 = shift(yhi, ROW, 8, 1)
        yh1 = shift(ylo, ROW, 8, -1)
        operands = (pot, xl1, xh1, yl1, yh1, nu, scale, forcing)
        if outer_index < ITERS - 1:
            pot, msg = call(
                sweep_two_gather_body,
                (sds(brick), sds((128, 128))),
                operands + (hot, rows_col, weights_col),
                scratch=scratch,
            )
        else:
            pot = call(sweep_two_body, sds(brick), operands, scratch=scratch)

    lower, upper = pot[0:2], pot[2:4]
    mine = jnp.where(h == 0, lower, upper)
    theirs = jnp.where(h == 0, upper, lower)
    hi = lax.reduce_precision(flux[1], 8, 7)
    final = swap_h(
        jnp.concatenate(
            [
                theirs.reshape(512, 128).astype(BF16),
                hi.astype(BF16),
                (flux[1] - hi).astype(BF16),
            ]
        )
    ).astype(F32)
    theirs = final[:512].reshape(2, LY, EH, LZ)
    out = jnp.where(
        h == 0, jnp.concatenate([mine, theirs], axis=2), jnp.concatenate([theirs, mine], axis=2)
    )
    flux_out = by_h(h, flux[0], final[512:528] + final[528:544])
    return out.transpose(2, 0, 1, 3), flux_out


def solution(mesh):
    fine = Mesh(mesh.devices.reshape(4, 8, 2, 4, 2), ("x", "y", "h", "z", "c"))
    vol, src = ("x", "y", "h"), ("z", "c")
    return jax.shard_map(
        per_device,
        mesh=fine,
        in_specs=(
            P(None, vol, src, None),
            P(None, vol, src, None),
            P(vol, src, None),
            P(vol, src, None),
            P(vol, src, None),
            P(vol, src, None),
            P(vol, src, None),
            P(None, vol),
            P(None, src),
        ),
        out_specs=(P(None, vol, src, None), P(None, vol + src)),
        check_vma=False,
    )
```

```python
import jax
import jax.numpy as jnp
from jax import lax
from jax.experimental import pallas as pl
from jax.experimental.pallas import tpu as pltpu
from jax.sharding import Mesh
from jax.sharding import PartitionSpec as P

P_SIZE = 65536
ITERS = 2
NU_BASE = (1.0, 0.05, 0.4)
NU_SATURATION = (0.0, 0.9, 0.3)
RELAXATION = 0.8
SOFTENING = 0.05

F32 = jnp.float32
BF16 = jnp.bfloat16
NXY = 32
EH = 16
LX, LY, LZ = 4, 16, 128
KERNEL_VMEM = 60 << 20
VM = pl.BlockSpec(memory_space=pltpu.VMEM)
SM = pl.BlockSpec(memory_space=pltpu.SMEM)
PLANE = ("x", "y")
ROW = ("z", "c")


def sds(shape, dtype=F32):
    return jax.ShapeDtypeStruct(shape, dtype)


def call(body, out_shape, args, smem=(), scratch=(), flops=2_000_000, nbytes=2_000_000):
    return pl.pallas_call(
        body,
        out_shape=out_shape,
        in_specs=[SM if i in smem else VM for i in range(len(args))],
        out_specs=jax.tree.map(lambda _: VM, out_shape),
        scratch_shapes=list(scratch),
        compiler_params=pltpu.CompilerParams(vmem_limit_bytes=8 << 20),
        cost_estimate=pl.CostEstimate(flops=flops, bytes_accessed=nbytes, transcendentals=0),
    )(*args)


def split3(value):
    one = value.astype(BF16).astype(F32)
    rest = value - one
    two = rest.astype(BF16).astype(F32)
    return one, two, rest - two


def augmented(points, is_target):
    length = points.shape[1]
    shifted = jnp.concatenate([points - 0.5, jnp.zeros((5, length), F32)])
    norm = jnp.sum(shifted * shifted, axis=0, keepdims=True)
    if is_target:
        norm = norm + SOFTENING * SOFTENING
    norms = split3(norm)
    parts = split3(shifted)
    index = lax.broadcasted_iota(jnp.int32, (8, length), 0)
    first = 0 if is_target else 3
    extra = jnp.where(index < 6, 1.0, 0.0)
    for i in range(3):
        extra = jnp.where(index == first + i, norms[i], extra)
    rows = []
    for i in range(3):
        for j in range(3):
            rows.append(-2.0 * parts[i] if is_target else parts[j])
    return jnp.concatenate(rows + [extra, jnp.zeros((48, length), F32)])


def kernel_matrix_body(t_ref, s_ref, out_ref, turned_ref, aug_ref):
    @pl.when(pl.program_id(0) == 0)
    def _():
        aug_ref[...] = augmented(t_ref[...], True).astype(BF16)

    sources = augmented(s_ref[...], False)
    for i in range(4):
        pieces = [sources[:, (2 * i + k) * 128 : (2 * i + k + 1) * 128].T for k in range(2)]
        turned = jnp.concatenate(pieces).astype(BF16)
        at = slice(i * 256, (i + 1) * 256)
        turned_ref[at, :] = turned
        dist_sq = jnp.dot(turned, aug_ref[...], preferred_element_type=F32)
        out_ref[at, :] = lax.rsqrt(dist_sq).astype(BF16)


def kernel_matrix(targets, sources):
    return pl.pallas_call(
        kernel_matrix_body,
        grid=(8,),
        out_shape=(sds((8192, 1024), BF16), sds((8192, 128), BF16)),
        in_specs=[
            pl.BlockSpec((3, 1024), lambda i: (0, 0)),
            pl.BlockSpec((3, 1024), lambda i: (0, i)),
        ],
        out_specs=(
            pl.BlockSpec((1024, 1024), lambda i: (i, 0)),
            pl.BlockSpec((1024, 128), lambda i: (i, 0)),
        ),
        scratch_shapes=[pltpu.VMEM((128, 1024), BF16)],
        compiler_params=pltpu.CompilerParams(vmem_limit_bytes=KERNEL_VMEM),
        cost_estimate=pl.CostEstimate(
            flops=2_000_000_000, bytes_accessed=20_000_000, transcendentals=8_400_000
        ),
    )(targets, sources)


def density_body(arr, owner_hot, msg):
    turned = arr[...].T
    dens = []
    for wl in range(2):
        total = jnp.zeros((EH, 128), F32)
        for vl in range(2):
            q = vl * 2 + wl
            rows = turned[q * EH : (q + 1) * EH]
            parts = jnp.concatenate(split3(rows)).astype(BF16)
            found = jnp.dot(
                parts, owner_hot[q * 128 : (q + 1) * 128, :], preferred_element_type=F32
            )
            total = total + found[:EH] + found[EH : 2 * EH] + found[2 * EH :]
        dens.append(total)
    out = jnp.concatenate(dens).astype(BF16)
    for peer in range(NXY):
        msg[peer] = out


FLUX_STEPS = 4
FLUX_ROWS = 8192 // FLUX_STEPS


def flux_body(arr, t_ref, ka, kb, kc, kd, turned_ref, out_ref, aug_ref, acc_ref):
    step = pl.program_id(0)

    @pl.when(step == 0)
    def _():
        aug_ref[...] = augmented(t_ref[...], True).astype(BF16)
        acc_ref[...] = jnp.zeros_like(acc_ref)

    pieces = []
    for i in range(FLUX_ROWS // 256):
        pieces += [arr[i, :EH], arr[i, EH:]]
    dens = jnp.concatenate(pieces, axis=1)
    depth = FLUX_ROWS // 4
    for c in range(2):
        at = slice(c * 512, (c + 1) * 512)
        dist_sq = jnp.dot(turned_ref[...], aug_ref[:, at], preferred_element_type=F32)
        k1 = lax.rsqrt(dist_sq).astype(BF16)
        acc_ref[1, :, at] += jnp.dot(dens, k1, preferred_element_type=F32)
        total = acc_ref[0, :, at]
        for part, k_ref in enumerate((ka, kb, kc, kd)):
            total = total + jnp.dot(
                dens[:, part * depth : (part + 1) * depth],
                k_ref[:, at],
                preferred_element_type=F32,
            )
        acc_ref[0, :, at] = total

    @pl.when(step == FLUX_STEPS - 1)
    def _():
        for half in range(2):
            for part in range(8):
                out_ref[part, half] = acc_ref[half, :, part * 128 : (part + 1) * 128] * (
                    float(P_SIZE) ** (-0.5)
                )


def stored_part(part):
    return pl.BlockSpec((FLUX_ROWS // 4, 1024), lambda i: (i * 4 + part, 0))


def partial_flux(arrived, targets, k0, turned):
    return pl.pallas_call(
        flux_body,
        grid=(FLUX_STEPS,),
        out_shape=sds((8, 2, EH, 128)),
        in_specs=[
            pl.BlockSpec((FLUX_ROWS // 256, 2 * EH, 128), lambda i: (i, 0, 0)),
            pl.BlockSpec((3, 1024), lambda i: (0, 0)),
            *[stored_part(part) for part in range(4)],
            pl.BlockSpec((FLUX_ROWS, 128), lambda i: (i, 0)),
        ],
        out_specs=pl.BlockSpec((8, 2, EH, 128), lambda i: (0, 0, 0, 0)),
        scratch_shapes=[pltpu.VMEM((128, 1024), BF16), pltpu.VMEM((2, EH, 1024), F32)],
        compiler_params=pltpu.CompilerParams(vmem_limit_bytes=KERNEL_VMEM),
        cost_estimate=pl.CostEstimate(
            flops=4_000_000_000, bytes_accessed=20_000_000, transcendentals=8_400_000
        ),
    )(arrived, targets, k0, k0, k0, k0, turned)


def owner_body(flags_ref, parts_ref, owner_hot, flux_ref, msg_ref):
    total = parts_ref[0]
    for part in range(1, 8):
        total = total + parts_ref[part]
    flux_ref[...] = total
    swapped = flags_ref[4] == 1
    blocks = (
        jnp.where(swapped, total[1], total[0]),
        jnp.where(swapped, total[0], total[1]),
    )
    nt = (((1,), (1,)), ((), ()))
    out = jnp.zeros((128, 128), F32)
    for q in range(4):
        above_rows = [jnp.zeros((EH * q, 128), F32)] if q else []
        rows = jnp.concatenate(
            above_rows + [blocks[q % 2], jnp.zeros((128 - EH * (q + 1), 128), F32)]
        )
        for piece in split3(rows):
            out = out + lax.dot_general(
                owner_hot[q * 128 : (q + 1) * 128, :],
                piece.astype(BF16),
                nt,
                preferred_element_type=F32,
            )
    msg_ref[...] = out


def lane_iota():
    return lax.broadcasted_iota(jnp.int32, (EH, LZ), 1)


def below(value, lane, edge):
    return jnp.where(lane == 0, edge, pltpu.roll(value, 1, 1))


def above(value, lane, edge):
    return jnp.where(lane == LZ - 1, edge, pltpu.roll(value, LZ - 1, 1))


def nu_body(
    flags_ref, pot, xl, xh, yl, yh, mo, mxl, mxh, myl, myh, nu, scale, pp
):
    pp[2:6, 2:18] = pot[...]
    pp[0:2, 2:18] = xl[...].astype(F32)
    pp[6:8, 2:18] = xh[...].astype(F32)
    pp[1:7, 0:2] = yl[...].astype(F32)
    pp[1:7, 18:20] = yh[...].astype(F32)
    lane = lane_iota()

    def nu_at(x, y, ids):
        center = pp[x, y]
        gx = pp[x + 1, y] - pp[x - 1, y]
        gy = pp[x, y + 1] - pp[x, y - 1]
        gz = above(center, lane, 0.0) - below(center, lane, 0.0)
        grad_sq = 0.25 * (gx * gx + gy * gy + gz * gz)
        base = jnp.where(ids == 0, NU_BASE[0], jnp.where(ids == 1, NU_BASE[1], NU_BASE[2]))
        slope = jnp.where(
            ids == 0, NU_SATURATION[0], jnp.where(ids == 1, NU_SATURATION[1], NU_SATURATION[2])
        )
        return base + slope * (grad_sq / (1.0 + grad_sq))

    def own_rows(y, carry):
        for x in range(LX):
            nu[x + 1, y + 1] = nu_at(x + 2, y + 2, mo[x, pl.ds(y, 1), :])
        nu[0, y + 1] = jnp.where(
            flags_ref[0] == 1, nu[1, y + 1], nu_at(1, y + 2, mxl[pl.ds(y, 1), :])
        )
        nu[5, y + 1] = jnp.where(
            flags_ref[1] == 1, nu[4, y + 1], nu_at(6, y + 2, mxh[pl.ds(y, 1), :])
        )
        return carry

    lax.fori_loop(0, LY, own_rows, 0)
    for x in range(LX):
        nu[x + 1, 0] = jnp.where(
            flags_ref[2] == 1, nu[x + 1, 1], nu_at(x + 2, 1, myl[x : x + 1, :])
        )
        nu[x + 1, 17] = jnp.where(
            flags_ref[3] == 1, nu[x + 1, 16], nu_at(x + 2, 18, myh[x : x + 1, :])
        )

    def scale_rows(y, carry):
        for x in range(LX):
            own = nu[x + 1, y + 1]
            total = (
                nu[x, y + 1]
                + nu[x + 2, y + 1]
                + nu[x + 1, y]
                + nu[x + 1, y + 2]
                + below(own, lane, own)
                + above(own, lane, own)
            )
            scale[x, y] = RELAXATION / (3.0 * own + 0.5 * total)
        return carry

    lax.fori_loop(0, LY, scale_rows, 0)


def relaxed(p, px, py, nu, scale, forcing, x, y, lane):
    center = p[x + px, y + py]
    own = nu[x + 1, y + 1]
    around = (
        (p[x + px - 1, y + py], nu[x, y + 1]),
        (p[x + px + 1, y + py], nu[x + 2, y + 1]),
        (p[x + px, y + py - 1], nu[x + 1, y]),
        (p[x + px, y + py + 1], nu[x + 1, y + 2]),
        (below(center, lane, 0.0), pltpu.roll(own, 1, 1)),
        (above(center, lane, 0.0), pltpu.roll(own, LZ - 1, 1)),
    )
    total = around[0][0] * (own + around[0][1])
    for value, other in around[1:]:
        total = total + value * (own + other)
    return (1.0 - RELAXATION) * center + scale[x, y] * (forcing + 0.5 * total)


def sweep_one_body(
    arr, hot, lanes_ref, exc, pot_in, xl, xh, yl, yh, nu, scale,
    pot, forcing, xlo, xhi, ylo, yhi, p,
):
    turned = arr[...].T
    lane = lane_iota()
    p[1:5, 1:17] = pot_in[...]
    p[0:1, 1:17] = xl[1:2].astype(F32)
    p[5:6, 1:17] = xh[0:1].astype(F32)
    p[1:5, 0:1] = yl[1:5, 1:2].astype(F32)
    p[1:5, 17:18] = yh[1:5, 0:1].astype(F32)
    slots = jnp.concatenate([turned[q * EH : (q + 1) * EH] for q in range(4)], axis=1)
    slots = slots * lanes_ref[1:2, :]
    hi = slots.astype(BF16).astype(F32)
    low = slots - hi
    cell_row = lanes_ref[0:1, :]
    for group in range(8):
        masks = [cell_row == float(group * 8 + i) for i in range(8)]
        surface = jnp.zeros((128, 128), F32)
        for piece in (hi, low):
            stacked = jnp.concatenate([jnp.where(m, piece, 0.0) for m in masks]).astype(BF16)
            surface = surface + jnp.dot(stacked, hot[...], preferred_element_type=F32)
        x = group // 2
        for i in range(8):
            y = (group % 2) * 8 + i
            forcing[x, y] = exc[x, y] + surface[i * EH : (i + 1) * EH]

    def rows(y, carry):
        for x in range(LX):
            pot[x, y] = relaxed(p, 1, 1, nu, scale, forcing[x, y], x, y, lane)
        return carry

    lax.fori_loop(0, LY, rows, 0)
    xlo[...] = pot[0:1].astype(xlo.dtype)
    xhi[...] = pot[LX - 1 : LX].astype(xhi.dtype)
    ylo[...] = pot[:, 0:1].astype(ylo.dtype)
    yhi[...] = pot[:, LY - 1 : LY].astype(yhi.dtype)


def sweep_two_body(pot_in, xl, xh, yl, yh, nu, scale, forcing, pot, p):
    p[1:5, 1:17] = pot_in[...]
    p[0:1, 1:17] = xl[...].astype(F32)
    p[5:6, 1:17] = xh[...].astype(F32)
    p[1:5, 0:1] = yl[...].astype(F32)
    p[1:5, 17:18] = yh[...].astype(F32)
    lane = lane_iota()

    def rows(y, carry):
        for x in range(LX):
            pot[x, y] = relaxed(p, 1, 1, nu, scale, forcing[x, y], x, y, lane)
        return carry

    lax.fori_loop(0, LY, rows, 0)


def gather_traces(pot, hot, rows_ref, weight_ref, msg):
    nt = (((1,), (1,)), ((), ()))
    taken = jnp.zeros((512, 128), F32)
    for group in range(8):
        x, y = group // 2, (group % 2) * 8
        block = pot[x, y : y + 8].reshape(128, LZ)
        value = jnp.zeros((512, 128), F32)
        for piece in split3(block):
            value = value + lax.dot_general(
                hot[...], piece.astype(BF16), nt, preferred_element_type=F32
            )
        taken = jnp.where(rows_ref[...] == float(group * 8), value, taken)
    taken = taken * weight_ref[...]
    for shift_by in (64, 32, 16):
        taken = taken + pltpu.roll(taken, shift_by, 1)
    lane_group = lax.broadcasted_iota(jnp.int32, (128, 128), 1) // EH
    out = jnp.zeros((128, 128), F32)
    for q in range(4):
        out = jnp.where(lane_group == q, taken[q * 128 : (q + 1) * 128], out)
    msg[...] = out


def tables_body(cell, count, weight, panel, points, material, out):
    lane = lax.broadcasted_iota(jnp.int32, (256, 128), 1)
    index = lax.broadcasted_iota(jnp.int32, (256, 128), 0)
    rows = jnp.concatenate(
        [
            cell[0].astype(F32),
            weight[0],
            panel[0].astype(F32),
            jnp.zeros((5, 256), F32),
        ]
    )
    parts = jnp.concatenate(split3(rows)).astype(BF16)
    counts = jnp.broadcast_to(count[0].astype(F32), (16, 64)).astype(BF16)
    rank = (lax.broadcasted_iota(jnp.int32, (1, 128), 1) % 4).astype(F32)
    picked = []
    for b in range(2):
        take = jnp.where(index == (lane // 4) * 8 + b * 4 + lane % 4, 1.0, 0.0).astype(BF16)
        found = jnp.dot(parts, take, preferred_element_type=F32)
        found = found[:8] + found[8:16] + found[16:]
        spread = jnp.where(index == (lane // 4) * 2 + b, 1.0, 0.0)[:64].astype(BF16)
        live = jnp.dot(counts, spread, preferred_element_type=F32)[0:1]
        picked.append((found[0:1], jnp.where(rank < live, found[1:2], 0.0), found[2:3]))
    for kind in range(3):
        for b in range(2):
            out[kind * 2 + b : kind * 2 + b + 1, :] = picked[b][kind]
    out[6:8, :] = jnp.zeros((2, 128), F32)
    for component in range(3):
        for j in range(8):
            row = 8 + component * 8 + j
            out[row : row + 1, :] = points[component : component + 1, j * 128 : (j + 1) * 128]
    for x in range(2):
        out[32 + x * LY : 32 + (x + 1) * LY, :] = material[x].astype(F32)


def tables_gather_body(
    flags_ref, own, other, pot, msg, hot, rows_ref, weight_ref, owner_hot, lanes_ref
):
    swapped = flags_ref[4] == 1
    first = jnp.where(swapped, other[...], own[...])
    second = jnp.where(swapped, own[...], other[...])
    lane = lax.broadcasted_iota(jnp.int32, (128, 128), 1)
    lane_f = lane.astype(F32)
    group_f = (lane // EH).astype(F32)

    def column(row):
        return jnp.broadcast_to(row, (128, 128)).T

    for vl, table in enumerate((first, second)):
        for wl in range(2):
            q = vl * 2 + wl
            at = slice(q * 128, (q + 1) * 128)
            cell_row = jnp.floor(table[wl : wl + 1] * (1.0 / LZ))
            depth = table[wl : wl + 1] - cell_row * LZ
            cell_row = cell_row + 32.0 * vl
            lanes_ref[:, at] = jnp.concatenate(
                [cell_row, table[2 + wl : 3 + wl], jnp.zeros((6, 128), F32)]
            )
            hot[at, :] = jnp.where(column(depth) == lane_f, 1.0, 0.0).astype(BF16)
            rows_ref[at, :] = column(cell_row) - group_f
            weight_ref[at, :] = column(table[2 + wl : 3 + wl])
            owned = (first, second)[wl][4 + vl : 5 + vl]
            owner_hot[at, :] = jnp.where(column(owned) == lane_f, 1.0, 0.0).astype(BF16)
    gather_traces(pot, hot, rows_ref, weight_ref, msg)


def sweep_two_gather_body(
    pot_in, xl, xh, yl, yh, nu, scale, forcing, hot, rows_ref, weight_ref, pot, msg, p
):
    sweep_two_body(pot_in, xl, xh, yl, yh, nu, scale, forcing, pot, p)
    gather_traces(pot, hot, rows_ref, weight_ref, msg)


def shift(value, axes, count, step):
    pairs = [(i, i + step) for i in range(count) if 0 <= i + step < count]
    return lax.ppermute(value, axes, pairs)


def swap_h(value):
    return lax.ppermute(value, "h", [(0, 1), (1, 0)])


def by_h(h, own, other):
    return jnp.where(h == 0, jnp.concatenate([own, other]), jnp.concatenate([other, own]))


def halved(value, h):
    turned = value.transpose(1, 2, 0, 3)
    low, high = turned[:, :, :EH], turned[:, :, EH:]
    return jnp.where(h == 0, low, high), jnp.where(h == 0, high, low)


def per_device(
    excitation,
    start,
    material,
    face_cell,
    face_count,
    face_weight,
    slot_panel,
    target_points,
    source_points,
):
    h = lax.axis_index("h")
    plane = lax.axis_index(PLANE)
    row = lax.axis_index(ROW)
    flags = jnp.stack(
        [plane == 0, plane == NXY - 1, row == 0, row == 7, h == 1, h == 1, h == 1, h == 1]
    ).astype(jnp.int32)

    block = call(
        tables_body,
        sds((64, 128)),
        (face_cell, face_count, face_weight, slot_panel, target_points, material),
    )
    tables = block[:8]
    keep, give = halved(start, h)
    got = swap_h(jnp.concatenate([give.reshape(512, 128), block]))
    k0, turned = kernel_matrix(target_points, source_points)

    pot = by_h(h, keep, got[:512].reshape(2, LY, EH, LZ))
    mats = by_h(h, block[32:64].reshape(2, LY, LZ), got[544:576].reshape(2, LY, LZ))
    msg, hot, rows_col, weights_col, owner_hot, lanes = call(
        tables_gather_body,
        (
            sds((128, 128)),
            sds((512, 128), BF16),
            sds((512, 128)),
            sds((512, 128)),
            sds((512, 128), BF16),
            sds((8, 512)),
        ),
        (flags, tables, got[512:520], pot),
        smem=(0,),
    )
    their_targets = got[520:544].reshape(3, 1024)

    rims = None
    for outer_index in range(ITERS):
        if outer_index == 0:
            msg, coarse, late = lax.optimization_barrier((msg, pot, excitation))
            exc_keep, exc_give = halved(late, h)
            exc = by_h(h, exc_keep, swap_h(exc_give.astype(BF16)).astype(F32))
        else:
            msg, coarse = lax.optimization_barrier((msg, pot))
        coarse = coarse.astype(BF16)
        arrived = lax.all_to_all(msg.reshape(NXY, 4, 128), PLANE, 0, 0, tiled=True)
        dens = call(
            density_body, sds((NXY, 2 * EH, 128), BF16), (arrived.reshape(128, 128), owner_hot)
        )
        dens = lax.all_to_all(dens, PLANE, 0, 0, tiled=True)

        up, down = coarse[2:4].reshape(512, 128), coarse[0:2].reshape(512, 128)
        if outer_index == 0:
            up = jnp.concatenate([up, mats[3].astype(BF16)])
            down = jnp.concatenate([down, mats[0].astype(BF16)])
        xl = shift(up, PLANE, NXY, 1)
        xh = shift(down, PLANE, NXY, -1)
        parts = partial_flux(dens, their_targets, k0, turned)
        xl, xh, parts = lax.optimization_barrier((xl, xh, parts))
        xl_pot = xl[:512].reshape(2, LY, EH, LZ)
        xh_pot = xh[:512].reshape(2, LY, EH, LZ)

        def side(part):
            rows = jnp.concatenate([xl_pot[1:2, part], coarse[:, part], xh_pot[0:1, part]])
            return rows.reshape(6 * 2 * EH, LZ)

        up, down = side(slice(14, 16)), side(slice(0, 2))
        if outer_index == 0:
            pad = jnp.zeros((12, 128), BF16)
            up = jnp.concatenate([up, mats[:, 15].astype(BF16), pad])
            down = jnp.concatenate([down, mats[:, 0].astype(BF16), pad])
        yl = shift(up, ROW, 8, 1)
        yh = shift(down, ROW, 8, -1)
        parts = lax.all_to_all(parts, ROW, 0, 0, tiled=True)
        flux, slots = call(
            owner_body, (sds((2, EH, 128)), sds((128, 128))), (flags, parts, owner_hot), smem=(0,)
        )
        yl, yh, slots = lax.optimization_barrier((yl, yh, slots))
        back = lax.all_to_all(slots.reshape(NXY, 4, 128), PLANE, 0, 0, tiled=True)
        if outer_index == 0:
            rims = tuple(v.astype(F32) for v in (xl[512:], xh[512:], yl[192:], yh[192:]))
        scratch = (pltpu.VMEM((6, 18, EH, LZ), F32),)
        halos = (
            xl_pot,
            xh_pot,
            yl[:192].reshape(6, 2, EH, LZ),
            yh[:192].reshape(6, 2, EH, LZ),
        )
        nu, scale = call(
            nu_body,
            (sds((6, 18, EH, LZ)), sds((LX, LY, EH, LZ))),
            (flags, pot, *halos, mats, *rims),
            smem=(0,),
            scratch=(pltpu.VMEM((8, 20, EH, LZ), F32),),
        )

        brick = (LX, LY, EH, LZ)
        pot, forcing, xlo, xhi, ylo, yhi = call(
            sweep_one_body,
            (
                sds(brick),
                sds(brick),
                sds((1, LY, EH, LZ), BF16),
                sds((1, LY, EH, LZ), BF16),
                sds((LX, 1, EH, LZ), BF16),
                sds((LX, 1, EH, LZ), BF16),
            ),
            (back.reshape(128, 128), hot, lanes, exc, pot, *halos, nu, scale),
            scratch=scratch,
        )
        xl1 = shift(xhi, PLANE, NXY, 1)
        xh1 = shift(xlo, PLANE, NXY, -1)
        yl1 = shift(yhi, ROW, 8, 1)
        yh1 = shift(ylo, ROW, 8, -1)
        operands = (pot, xl1, xh1, yl1, yh1, nu, scale, forcing)
        if outer_index < ITERS - 1:
            pot, msg = call(
                sweep_two_gather_body,
                (sds(brick), sds((128, 128))),
                operands + (hot, rows_col, weights_col),
                scratch=scratch,
            )
        else:
            pot = call(sweep_two_body, sds(brick), operands, scratch=scratch)

    lower, upper = pot[0:2], pot[2:4]
    mine = jnp.where(h == 0, lower, upper)
    theirs = jnp.where(h == 0, upper, lower)
    hi = lax.reduce_precision(flux[1], 8, 7)
    final = swap_h(
        jnp.concatenate(
            [
                theirs.reshape(512, 128).astype(BF16),
                hi.astype(BF16),
                (flux[1] - hi).astype(BF16),
            ]
        )
    ).astype(F32)
    theirs = final[:512].reshape(2, LY, EH, LZ)
    out = jnp.where(
        h == 0, jnp.concatenate([mine, theirs], axis=2), jnp.concatenate([theirs, mine], axis=2)
    )
    flux_out = by_h(h, flux[0], final[512:528] + final[528:544])
    return out.transpose(2, 0, 1, 3), flux_out


def solution(mesh):
    fine = Mesh(mesh.devices.reshape(4, 8, 2, 4, 2), ("x", "y", "h", "z", "c"))
    vol, src = ("x", "y", "h"), ("z", "c")
    return jax.shard_map(
        per_device,
        mesh=fine,
        in_specs=(
            P(None, vol, src, None),
            P(None, vol, src, None),
            P(vol, src, None),
            P(vol, src, None),
            P(vol, src, None),
            P(vol, src, None),
            P(vol, src, None),
            P(None, vol),
            P(None, src),
        ),
        out_specs=(P(None, vol, src, None), P(None, vol + src)),
        check_vma=False,
    )
```

```python
import jax
import jax.numpy as jnp
from jax import lax
from jax.experimental import pallas as pl
from jax.experimental.pallas import tpu as pltpu
from jax.sharding import Mesh
from jax.sharding import PartitionSpec as P

P_SIZE = 65536
ITERS = 2
NU_BASE = (1.0, 0.05, 0.4)
NU_SATURATION = (0.0, 0.9, 0.3)
RELAXATION = 0.8
SOFTENING = 0.05

F32 = jnp.float32
BF16 = jnp.bfloat16
NXY = 32
EH = 16
LX, LY, LZ = 4, 16, 128
KERNEL_VMEM = 60 << 20
VM = pl.BlockSpec(memory_space=pltpu.VMEM)
SM = pl.BlockSpec(memory_space=pltpu.SMEM)
PLANE = ("x", "y")
ROW = ("z", "c")


def sds(shape, dtype=F32):
    return jax.ShapeDtypeStruct(shape, dtype)


def call(body, out_shape, args, smem=(), scratch=(), flops=2_000_000, nbytes=2_000_000, room=8 << 20):
    return pl.pallas_call(
        body,
        out_shape=out_shape,
        in_specs=[SM if i in smem else VM for i in range(len(args))],
        out_specs=jax.tree.map(lambda _: VM, out_shape),
        scratch_shapes=list(scratch),
        compiler_params=pltpu.CompilerParams(vmem_limit_bytes=room),
        cost_estimate=pl.CostEstimate(flops=flops, bytes_accessed=nbytes, transcendentals=0),
    )(*args)


def split3(value):
    one = value.astype(BF16).astype(F32)
    rest = value - one
    two = rest.astype(BF16).astype(F32)
    return one, two, rest - two


def augmented(points, is_target):
    length = points.shape[1]
    shifted = jnp.concatenate([points - 0.5, jnp.zeros((5, length), F32)])
    norm = jnp.sum(shifted * shifted, axis=0, keepdims=True)
    if is_target:
        norm = norm + SOFTENING * SOFTENING
    norms = split3(norm)
    parts = split3(shifted)
    index = lax.broadcasted_iota(jnp.int32, (8, length), 0)
    first = 0 if is_target else 3
    extra = jnp.where(index < 6, 1.0, 0.0)
    for i in range(3):
        extra = jnp.where(index == first + i, norms[i], extra)
    rows = []
    for i in range(3):
        for j in range(3):
            rows.append(-2.0 * parts[i] if is_target else parts[j])
    return jnp.concatenate(rows + [extra, jnp.zeros((48, length), F32)])


def kernel_matrix_body(t_ref, s_ref, out_ref, turned_ref, aug_ref):
    @pl.when(pl.program_id(0) == 0)
    def _():
        aug_ref[...] = augmented(t_ref[...], True).astype(BF16)

    sources = augmented(s_ref[...], False)
    for i in range(4):
        pieces = [sources[:, (2 * i + k) * 128 : (2 * i + k + 1) * 128].T for k in range(2)]
        turned = jnp.concatenate(pieces).astype(BF16)
        at = slice(i * 256, (i + 1) * 256)
        turned_ref[at, :] = turned
        dist_sq = jnp.dot(turned, aug_ref[...], preferred_element_type=F32)
        out_ref[at, :] = lax.rsqrt(dist_sq).astype(BF16)


def kernel_matrix(targets, sources):
    return pl.pallas_call(
        kernel_matrix_body,
        grid=(8,),
        out_shape=(sds((8192, 1024), BF16), sds((8192, 128), BF16)),
        in_specs=[
            pl.BlockSpec((3, 1024), lambda i: (0, 0)),
            pl.BlockSpec((3, 1024), lambda i: (0, i)),
        ],
        out_specs=(
            pl.BlockSpec((1024, 1024), lambda i: (i, 0)),
            pl.BlockSpec((1024, 128), lambda i: (i, 0)),
        ),
        scratch_shapes=[pltpu.VMEM((128, 1024), BF16)],
        compiler_params=pltpu.CompilerParams(vmem_limit_bytes=KERNEL_VMEM),
        cost_estimate=pl.CostEstimate(
            flops=2_000_000_000, bytes_accessed=20_000_000, transcendentals=8_400_000
        ),
    )(targets, sources)


def density_body(arr, owner_hot, msg):
    turned = arr[...].T
    dens = []
    for wl in range(2):
        total = jnp.zeros((EH, 128), F32)
        for vl in range(2):
            q = vl * 2 + wl
            rows = turned[q * EH : (q + 1) * EH]
            parts = jnp.concatenate(split3(rows)).astype(BF16)
            found = jnp.dot(
                parts, owner_hot[q * 128 : (q + 1) * 128, :], preferred_element_type=F32
            )
            total = total + found[:EH] + found[EH : 2 * EH] + found[2 * EH :]
        dens.append(total)
    out = jnp.concatenate(dens).astype(BF16)
    for peer in range(NXY):
        msg[peer] = out


FLUX_STEPS = 4
FLUX_ROWS = 8192 // FLUX_STEPS


def flux_body(arr, t_ref, ka, kb, kc, kd, turned_ref, out_ref, aug_ref, acc_ref):
    step = pl.program_id(0)

    @pl.when(step == 0)
    def _():
        aug_ref[...] = augmented(t_ref[...], True).astype(BF16)
        acc_ref[...] = jnp.zeros_like(acc_ref)

    pieces = []
    for i in range(FLUX_ROWS // 256):
        pieces += [arr[i, :EH], arr[i, EH:]]
    dens = jnp.concatenate(pieces, axis=1)
    depth = FLUX_ROWS // 4
    for c in range(2):
        at = slice(c * 512, (c + 1) * 512)
        dist_sq = jnp.dot(turned_ref[...], aug_ref[:, at], preferred_element_type=F32)
        k1 = lax.rsqrt(dist_sq).astype(BF16)
        acc_ref[1, :, at] += jnp.dot(dens, k1, preferred_element_type=F32)
        total = acc_ref[0, :, at]
        for part, k_ref in enumerate((ka, kb, kc, kd)):
            total = total + jnp.dot(
                dens[:, part * depth : (part + 1) * depth],
                k_ref[:, at],
                preferred_element_type=F32,
            )
        acc_ref[0, :, at] = total

    @pl.when(step == FLUX_STEPS - 1)
    def _():
        for half in range(2):
            for part in range(8):
                out_ref[part, half] = acc_ref[half, :, part * 128 : (part + 1) * 128] * (
                    float(P_SIZE) ** (-0.5)
                )


def stored_part(part):
    return pl.BlockSpec((FLUX_ROWS // 4, 1024), lambda i: (i * 4 + part, 0))


def partial_flux(arrived, targets, k0, turned):
    return pl.pallas_call(
        flux_body,
        grid=(FLUX_STEPS,),
        out_shape=sds((8, 2, EH, 128)),
        in_specs=[
            pl.BlockSpec((FLUX_ROWS // 256, 2 * EH, 128), lambda i: (i, 0, 0)),
            pl.BlockSpec((3, 1024), lambda i: (0, 0)),
            *[stored_part(part) for part in range(4)],
            pl.BlockSpec((FLUX_ROWS, 128), lambda i: (i, 0)),
        ],
        out_specs=pl.BlockSpec((8, 2, EH, 128), lambda i: (0, 0, 0, 0)),
        scratch_shapes=[pltpu.VMEM((128, 1024), BF16), pltpu.VMEM((2, EH, 1024), F32)],
        compiler_params=pltpu.CompilerParams(vmem_limit_bytes=KERNEL_VMEM),
        cost_estimate=pl.CostEstimate(
            flops=4_000_000_000, bytes_accessed=20_000_000, transcendentals=8_400_000
        ),
    )(arrived, targets, k0, k0, k0, k0, turned)


def owner_body(flags_ref, parts_ref, owner_hot, flux_ref, msg_ref):
    total = parts_ref[0]
    for part in range(1, 8):
        total = total + parts_ref[part]
    flux_ref[...] = total
    swapped = flags_ref[4] == 1
    blocks = (
        jnp.where(swapped, total[1], total[0]),
        jnp.where(swapped, total[0], total[1]),
    )
    nt = (((1,), (1,)), ((), ()))
    out = jnp.zeros((128, 128), F32)
    for q in range(4):
        above_rows = [jnp.zeros((EH * q, 128), F32)] if q else []
        rows = jnp.concatenate(
            above_rows + [blocks[q % 2], jnp.zeros((128 - EH * (q + 1), 128), F32)]
        )
        for piece in split3(rows):
            out = out + lax.dot_general(
                owner_hot[q * 128 : (q + 1) * 128, :],
                piece.astype(BF16),
                nt,
                preferred_element_type=F32,
            )
    msg_ref[...] = out


def lane_iota():
    return lax.broadcasted_iota(jnp.int32, (EH, LZ), 1)


def below(value, lane, edge):
    return jnp.where(lane == 0, edge, pltpu.roll(value, 1, 1))


def above(value, lane, edge):
    return jnp.where(lane == LZ - 1, edge, pltpu.roll(value, LZ - 1, 1))


def nu_body(
    flags_ref, pot, xl, xh, yl, yh, mo, mxl, mxh, myl, myh, nu, scale, pp
):
    pp[2:6, 2:18] = pot[...]
    pp[0:2, 2:18] = xl[...].astype(F32)
    pp[6:8, 2:18] = xh[...].astype(F32)
    pp[1:7, 0:2] = yl[...].astype(F32)
    pp[1:7, 18:20] = yh[...].astype(F32)
    lane = lane_iota()

    def nu_at(x, y, ids):
        center = pp[x, y]
        gx = pp[x + 1, y] - pp[x - 1, y]
        gy = pp[x, y + 1] - pp[x, y - 1]
        gz = above(center, lane, 0.0) - below(center, lane, 0.0)
        grad_sq = 0.25 * (gx * gx + gy * gy + gz * gz)
        base = jnp.where(ids == 0, NU_BASE[0], jnp.where(ids == 1, NU_BASE[1], NU_BASE[2]))
        slope = jnp.where(
            ids == 0, NU_SATURATION[0], jnp.where(ids == 1, NU_SATURATION[1], NU_SATURATION[2])
        )
        return base + slope * (grad_sq / (1.0 + grad_sq))

    def own_rows(y, carry):
        for x in range(LX):
            nu[x + 1, y + 1] = nu_at(x + 2, y + 2, mo[x, pl.ds(y, 1), :])
        nu[0, y + 1] = jnp.where(
            flags_ref[0] == 1, nu[1, y + 1], nu_at(1, y + 2, mxl[pl.ds(y, 1), :])
        )
        nu[5, y + 1] = jnp.where(
            flags_ref[1] == 1, nu[4, y + 1], nu_at(6, y + 2, mxh[pl.ds(y, 1), :])
        )
        return carry

    lax.fori_loop(0, LY, own_rows, 0)
    for x in range(LX):
        nu[x + 1, 0] = jnp.where(
            flags_ref[2] == 1, nu[x + 1, 1], nu_at(x + 2, 1, myl[x : x + 1, :])
        )
        nu[x + 1, 17] = jnp.where(
            flags_ref[3] == 1, nu[x + 1, 16], nu_at(x + 2, 18, myh[x : x + 1, :])
        )

    def scale_rows(y, carry):
        for x in range(LX):
            own = nu[x + 1, y + 1]
            total = (
                nu[x, y + 1]
                + nu[x + 2, y + 1]
                + nu[x + 1, y]
                + nu[x + 1, y + 2]
                + below(own, lane, own)
                + above(own, lane, own)
            )
            scale[x, y] = RELAXATION / (3.0 * own + 0.5 * total)
        return carry

    lax.fori_loop(0, LY, scale_rows, 0)


def relaxed(p, px, py, nu, scale, forcing, x, y, lane):
    center = p[x + px, y + py]
    own = nu[x + 1, y + 1]
    around = (
        (p[x + px - 1, y + py], nu[x, y + 1]),
        (p[x + px + 1, y + py], nu[x + 2, y + 1]),
        (p[x + px, y + py - 1], nu[x + 1, y]),
        (p[x + px, y + py + 1], nu[x + 1, y + 2]),
        (below(center, lane, 0.0), pltpu.roll(own, 1, 1)),
        (above(center, lane, 0.0), pltpu.roll(own, LZ - 1, 1)),
    )
    total = around[0][0] * (own + around[0][1])
    for value, other in around[1:]:
        total = total + value * (own + other)
    return (1.0 - RELAXATION) * center + scale[x, y] * (forcing + 0.5 * total)


def sweep_one_body(
    arr, hot, lanes_ref, exc, pot_in, xl, xh, yl, yh, nu, scale,
    pot, forcing, xlo, xhi, ylo, yhi, p,
):
    turned = arr[...].T
    lane = lane_iota()
    p[1:5, 1:17] = pot_in[...]
    p[0:1, 1:17] = xl[1:2].astype(F32)
    p[5:6, 1:17] = xh[0:1].astype(F32)
    p[1:5, 0:1] = yl[1:5, 1:2].astype(F32)
    p[1:5, 17:18] = yh[1:5, 0:1].astype(F32)
    slots = jnp.concatenate([turned[q * EH : (q + 1) * EH] for q in range(4)], axis=1)
    slots = slots * lanes_ref[1:2, :]
    hi = slots.astype(BF16).astype(F32)
    low = slots - hi
    cell_row = lanes_ref[0:1, :]
    for group in range(8):
        masks = [cell_row == float(group * 8 + i) for i in range(8)]
        surface = jnp.zeros((128, 128), F32)
        for piece in (hi, low):
            stacked = jnp.concatenate([jnp.where(m, piece, 0.0) for m in masks]).astype(BF16)
            surface = surface + jnp.dot(stacked, hot[...], preferred_element_type=F32)
        x = group // 2
        for i in range(8):
            y = (group % 2) * 8 + i
            forcing[x, y] = exc[x, y] + surface[i * EH : (i + 1) * EH]

    def rows(y, carry):
        for x in range(LX):
            pot[x, y] = relaxed(p, 1, 1, nu, scale, forcing[x, y], x, y, lane)
        return carry

    lax.fori_loop(0, LY, rows, 0)
    xlo[...] = pot[0:1].astype(xlo.dtype)
    xhi[...] = pot[LX - 1 : LX].astype(xhi.dtype)
    ylo[...] = pot[:, 0:1].astype(ylo.dtype)
    yhi[...] = pot[:, LY - 1 : LY].astype(yhi.dtype)


def sweep_two_body(pot_in, xl, xh, yl, yh, nu, scale, forcing, pot, p):
    p[1:5, 1:17] = pot_in[...]
    p[0:1, 1:17] = xl[...].astype(F32)
    p[5:6, 1:17] = xh[...].astype(F32)
    p[1:5, 0:1] = yl[...].astype(F32)
    p[1:5, 17:18] = yh[...].astype(F32)
    lane = lane_iota()

    def rows(y, carry):
        for x in range(LX):
            pot[x, y] = relaxed(p, 1, 1, nu, scale, forcing[x, y], x, y, lane)
        return carry

    lax.fori_loop(0, LY, rows, 0)


def gather_traces(pot, hot, rows_ref, weight_ref, msg):
    nt = (((1,), (1,)), ((), ()))
    taken = jnp.zeros((512, 128), F32)
    for group in range(8):
        x, y = group // 2, (group % 2) * 8
        block = pot[x, y : y + 8].reshape(128, LZ)
        value = jnp.zeros((512, 128), F32)
        for piece in split3(block):
            value = value + lax.dot_general(
                hot[...], piece.astype(BF16), nt, preferred_element_type=F32
            )
        taken = jnp.where(rows_ref[...] == float(group * 8), value, taken)
    taken = taken * weight_ref[...]
    for shift_by in (64, 32, 16):
        taken = taken + pltpu.roll(taken, shift_by, 1)
    lane_group = lax.broadcasted_iota(jnp.int32, (128, 128), 1) // EH
    out = jnp.zeros((128, 128), F32)
    for q in range(4):
        out = jnp.where(lane_group == q, taken[q * 128 : (q + 1) * 128], out)
    msg[...] = out


def tables_body(cell, count, weight, panel, points, material, out):
    lane = lax.broadcasted_iota(jnp.int32, (256, 128), 1)
    index = lax.broadcasted_iota(jnp.int32, (256, 128), 0)
    rows = jnp.concatenate(
        [
            cell[0].astype(F32),
            weight[0],
            panel[0].astype(F32),
            jnp.zeros((5, 256), F32),
        ]
    )
    parts = jnp.concatenate(split3(rows)).astype(BF16)
    counts = jnp.broadcast_to(count[0].astype(F32), (16, 64)).astype(BF16)
    rank = (lax.broadcasted_iota(jnp.int32, (1, 128), 1) % 4).astype(F32)
    picked = []
    for b in range(2):
        take = jnp.where(index == (lane // 4) * 8 + b * 4 + lane % 4, 1.0, 0.0).astype(BF16)
        found = jnp.dot(parts, take, preferred_element_type=F32)
        found = found[:8] + found[8:16] + found[16:]
        spread = jnp.where(index == (lane // 4) * 2 + b, 1.0, 0.0)[:64].astype(BF16)
        live = jnp.dot(counts, spread, preferred_element_type=F32)[0:1]
        picked.append((found[0:1], jnp.where(rank < live, found[1:2], 0.0), found[2:3]))
    for kind in range(3):
        for b in range(2):
            out[kind * 2 + b : kind * 2 + b + 1, :] = picked[b][kind]
    out[6:8, :] = jnp.zeros((2, 128), F32)
    for component in range(3):
        for j in range(8):
            row = 8 + component * 8 + j
            out[row : row + 1, :] = points[component : component + 1, j * 128 : (j + 1) * 128]
    for x in range(2):
        out[32 + x * LY : 32 + (x + 1) * LY, :] = material[x].astype(F32)


def tables_gather_body(
    flags_ref, own, other, pot, msg, hot, rows_ref, weight_ref, owner_hot, lanes_ref
):
    swapped = flags_ref[4] == 1
    first = jnp.where(swapped, other[...], own[...])
    second = jnp.where(swapped, own[...], other[...])
    lane = lax.broadcasted_iota(jnp.int32, (128, 128), 1)
    lane_f = lane.astype(F32)
    group_f = (lane // EH).astype(F32)

    def column(row):
        return jnp.broadcast_to(row, (128, 128)).T

    for vl, table in enumerate((first, second)):
        for wl in range(2):
            q = vl * 2 + wl
            at = slice(q * 128, (q + 1) * 128)
            cell_row = jnp.floor(table[wl : wl + 1] * (1.0 / LZ))
            depth = table[wl : wl + 1] - cell_row * LZ
            cell_row = cell_row + 32.0 * vl
            lanes_ref[:, at] = jnp.concatenate(
                [cell_row, table[2 + wl : 3 + wl], jnp.zeros((6, 128), F32)]
            )
            hot[at, :] = jnp.where(column(depth) == lane_f, 1.0, 0.0).astype(BF16)
            rows_ref[at, :] = column(cell_row) - group_f
            weight_ref[at, :] = column(table[2 + wl : 3 + wl])
            owned = (first, second)[wl][4 + vl : 5 + vl]
            owner_hot[at, :] = jnp.where(column(owned) == lane_f, 1.0, 0.0).astype(BF16)
    gather_traces(pot, hot, rows_ref, weight_ref, msg)


def sweep_two_gather_body(
    pot_in, xl, xh, yl, yh, nu, scale, forcing, hot, rows_ref, weight_ref, pot, msg, p
):
    sweep_two_body(pot_in, xl, xh, yl, yh, nu, scale, forcing, pot, p)
    gather_traces(pot, hot, rows_ref, weight_ref, msg)


def shift(value, axes, count, step):
    pairs = [(i, i + step) for i in range(count) if 0 <= i + step < count]
    return lax.ppermute(value, axes, pairs)


def swap_h(value):
    return lax.ppermute(value, "h", [(0, 1), (1, 0)])


def by_h(h, own, other):
    return jnp.where(h == 0, jnp.concatenate([own, other]), jnp.concatenate([other, own]))


def halved(value, h):
    turned = value.transpose(1, 2, 0, 3)
    low, high = turned[:, :, :EH], turned[:, :, EH:]
    return jnp.where(h == 0, low, high), jnp.where(h == 0, high, low)


def per_device(
    excitation,
    start,
    material,
    face_cell,
    face_count,
    face_weight,
    slot_panel,
    target_points,
    source_points,
):
    h = lax.axis_index("h")
    plane = lax.axis_index(PLANE)
    row = lax.axis_index(ROW)
    flags = jnp.stack(
        [plane == 0, plane == NXY - 1, row == 0, row == 7, h == 1, h == 1, h == 1, h == 1]
    ).astype(jnp.int32)

    block = call(
        tables_body,
        sds((64, 128)),
        (face_cell, face_count, face_weight, slot_panel, target_points, material),
        room=KERNEL_VMEM,
    )
    tables = block[:8]
    keep, give = halved(start, h)
    got = swap_h(jnp.concatenate([give.reshape(512, 128), block]))
    exc_keep, exc_give = halved(excitation, h)
    exc_got = swap_h(exc_give.astype(BF16))
    k0, turned = kernel_matrix(target_points, source_points)

    pot = by_h(h, keep, got[:512].reshape(2, LY, EH, LZ))
    mats = by_h(h, block[32:64].reshape(2, LY, LZ), got[544:576].reshape(2, LY, LZ))
    msg, hot, rows_col, weights_col, owner_hot, lanes = call(
        tables_gather_body,
        (
            sds((128, 128)),
            sds((512, 128), BF16),
            sds((512, 128)),
            sds((512, 128)),
            sds((512, 128), BF16),
            sds((8, 512)),
        ),
        (flags, tables, got[512:520], pot),
        smem=(0,),
    )
    their_targets = got[520:544].reshape(3, 1024)
    exc = by_h(h, exc_keep, exc_got.astype(F32))

    rims = None
    for outer_index in range(ITERS):
        arrived = lax.all_to_all(msg.reshape(NXY, 4, 128), PLANE, 0, 0, tiled=True)
        dens = call(
            density_body, sds((NXY, 2 * EH, 128), BF16), (arrived.reshape(128, 128), owner_hot)
        )
        dens, coarse = lax.optimization_barrier((dens, pot))
        coarse = coarse.astype(BF16)
        dens = lax.all_to_all(dens, PLANE, 0, 0, tiled=True)

        up, down = coarse[2:4].reshape(512, 128), coarse[0:2].reshape(512, 128)
        if outer_index == 0:
            up = jnp.concatenate([up, mats[3].astype(BF16)])
            down = jnp.concatenate([down, mats[0].astype(BF16)])
        xl = shift(up, PLANE, NXY, 1)
        xh = shift(down, PLANE, NXY, -1)
        parts = partial_flux(dens, their_targets, k0, turned)
        xl, xh, parts = lax.optimization_barrier((xl, xh, parts))
        xl_pot = xl[:512].reshape(2, LY, EH, LZ)
        xh_pot = xh[:512].reshape(2, LY, EH, LZ)

        def side(part):
            rows = jnp.concatenate([xl_pot[1:2, part], coarse[:, part], xh_pot[0:1, part]])
            return rows.reshape(6 * 2 * EH, LZ)

        up, down = side(slice(14, 16)), side(slice(0, 2))
        if outer_index == 0:
            pad = jnp.zeros((12, 128), BF16)
            up = jnp.concatenate([up, mats[:, 15].astype(BF16), pad])
            down = jnp.concatenate([down, mats[:, 0].astype(BF16), pad])
        yl = shift(up, ROW, 8, 1)
        yh = shift(down, ROW, 8, -1)
        parts = lax.all_to_all(parts, ROW, 0, 0, tiled=True)
        flux, slots = call(
            owner_body, (sds((2, EH, 128)), sds((128, 128))), (flags, parts, owner_hot), smem=(0,)
        )
        yl, yh, slots = lax.optimization_barrier((yl, yh, slots))
        back = lax.all_to_all(slots.reshape(NXY, 4, 128), PLANE, 0, 0, tiled=True)
        if outer_index == 0:
            rims = tuple(v.astype(F32) for v in (xl[512:], xh[512:], yl[192:], yh[192:]))
        scratch = (pltpu.VMEM((6, 18, EH, LZ), F32),)
        halos = (
            xl_pot,
            xh_pot,
            yl[:192].reshape(6, 2, EH, LZ),
            yh[:192].reshape(6, 2, EH, LZ),
        )
        nu, scale = call(
            nu_body,
            (sds((6, 18, EH, LZ)), sds((LX, LY, EH, LZ))),
            (flags, pot, *halos, mats, *rims),
            smem=(0,),
            scratch=(pltpu.VMEM((8, 20, EH, LZ), F32),),
        )

        brick = (LX, LY, EH, LZ)
        pot, forcing, xlo, xhi, ylo, yhi = call(
            sweep_one_body,
            (
                sds(brick),
                sds(brick),
                sds((1, LY, EH, LZ), BF16),
                sds((1, LY, EH, LZ), BF16),
                sds((LX, 1, EH, LZ), BF16),
                sds((LX, 1, EH, LZ), BF16),
            ),
            (back.reshape(128, 128), hot, lanes, exc, pot, *halos, nu, scale),
            scratch=scratch,
        )
        xl1 = shift(xhi, PLANE, NXY, 1)
        xh1 = shift(xlo, PLANE, NXY, -1)
        yl1 = shift(yhi, ROW, 8, 1)
        yh1 = shift(ylo, ROW, 8, -1)
        operands = (pot, xl1, xh1, yl1, yh1, nu, scale, forcing)
        if outer_index < ITERS - 1:
            pot, msg = call(
                sweep_two_gather_body,
                (sds(brick), sds((128, 128))),
                operands + (hot, rows_col, weights_col),
                scratch=scratch,
            )
        else:
            pot = call(sweep_two_body, sds(brick), operands, scratch=scratch)

    lower, upper = pot[0:2], pot[2:4]
    mine = jnp.where(h == 0, lower, upper)
    theirs = jnp.where(h == 0, upper, lower)
    hi = lax.reduce_precision(flux[1], 8, 7)
    final = swap_h(
        jnp.concatenate(
            [
                theirs.reshape(512, 128).astype(BF16),
                hi.astype(BF16),
                (flux[1] - hi).astype(BF16),
            ]
        )
    ).astype(F32)
    theirs = final[:512].reshape(2, LY, EH, LZ)
    out = jnp.where(
        h == 0, jnp.concatenate([mine, theirs], axis=2), jnp.concatenate([theirs, mine], axis=2)
    )
    flux_out = by_h(h, flux[0], final[512:528] + final[528:544])
    return out.transpose(2, 0, 1, 3), flux_out


def solution(mesh):
    fine = Mesh(mesh.devices.reshape(4, 8, 2, 4, 2), ("x", "y", "h", "z", "c"))
    vol, src = ("x", "y", "h"), ("z", "c")
    return jax.shard_map(
        per_device,
        mesh=fine,
        in_specs=(
            P(None, vol, src, None),
            P(None, vol, src, None),
            P(vol, src, None),
            P(vol, src, None),
            P(vol, src, None),
            P(vol, src, None),
            P(vol, src, None),
            P(None, vol),
            P(None, src),
        ),
        out_specs=(P(None, vol, src, None), P(None, vol + src)),
        check_vma=False,
    )
```
